32 devices in a mesh: seq: 8 (over z, x), head: 4 (over y, core).
Axes of the slice: x: 2, y: 2, z: 4, core: 2. Of those that a mesh axis runs over, the one named last changes fastest.
Arguments:
- queries: bfloat16 [2048, 4096], P('seq', 'head'), may hold values from -6 to 6
- key_rows: bfloat16 [2048, 4096], P('seq', 'head'), may hold values from -18 to 18
- values: bfloat16 [2048, 4096], P('seq', 'head'), may hold values from -6 to 6
- write_gate: float32 [2048, 32], P('seq', 'head'), may hold values from 0.05 to 1
- ridge_diag: float32 [32, 128], P('head'), may hold values from 0.1 to 4
- norm_gain: float32 [4096], replicated, may hold values from 0.5 to 1.5
- gate_logits: bfloat16 [2048, 4096], P(('seq', 'head')), may hold values from -8 to 8
Outputs:
- layer_out: bfloat16 [2048, 4096], P(('seq', 'head'))
The draws below stay inside these ranges and needn't reach their ends.
All inputs are finite; a program needn't handle non-finite values.
Results may differ from the reference program's by a relative error of at most 0.018.
Values may be sent and summed in bfloat16 or wider, within the bound.
No kernel may reach another device: no remote copies, remote signals or barrier semaphores. Data moves between devices by JAX's collectives and lax.ppermute only.
A program may use at most 128 MiB of HBM per device.

```python
import math
import jax
import jax.numpy as jnp
from jax import lax

HEADS = 32
DH = 128
D = 4096
TOK_DEV = 256
ITERS = 8
TOKENS = 2048


def draw_key_rows(key, part):
    key_scale = jax.random.fold_in(key, 11)
    key_base = jax.random.fold_in(key, 12)
    scales = jnp.exp(jax.random.uniform(key_scale, (HEADS * DH,), jnp.float32, math.log(0.1), math.log(3.0)))
    base = jax.random.truncated_normal(key_base, -6.0, 6.0, (TOKENS, HEADS * DH), jnp.float32)
    return (base * scales[None, :]).astype(jnp.bfloat16)


def steps_of(own_key, dims, pieces, smallest, high):
    loudness = 1.0
    for axis_at, shards_of in pieces:
        draws = jax.random.uniform(jax.random.fold_in(jax.random.fold_in(own_key, 6), axis_at), (shards_of,), jnp.float32, smallest / len(pieces), high / len(pieces))
        loudness = loudness * jnp.repeat(jnp.exp(draws), dims[axis_at] // shards_of).reshape((-1,) + (1,) * (len(dims) - 1 - axis_at))
    return loudness


def centred(key, extent, spread, most, cuts=(), dtype=jnp.bfloat16):
    values = spread * jax.random.normal(key, extent, jnp.float32)
    if cuts:
        values = values * steps_of(key, extent, cuts, -0.22, 0.18)
    return jnp.clip(values, -most, most).astype(dtype)


def setup_inputs(seed: int = 0) -> dict:
    arg_keys = jax.random.split(jax.random.key(seed), 8)
    queries = centred(arg_keys[0], (TOKENS, D), 1.0, 6.0, ((0, 8), (1, 4)))
    key_rows = draw_key_rows(jax.random.fold_in(arg_keys[7], 71), 0)
    values = centred(arg_keys[2], (TOKENS, D), 1.0, 6.0, ((0, 8), (1, 4)))
    write_gate = jnp.clip(0.05 + 0.95 * jax.random.uniform(arg_keys[3], (TOKENS, HEADS), jnp.float32) ** steps_of(arg_keys[3], (TOKENS, HEADS), ((0, 8), (1, 4)), -0.2, 0.2), 0.05, 1.0)
    ridge_diag = jnp.clip(jnp.exp(math.log(4.0) - 3.6888794 * jax.random.uniform(arg_keys[4], (HEADS, DH), jnp.float32) ** steps_of(arg_keys[4], (HEADS, DH), ((0, 4),), -0.2, 0.2)), 0.1, 4.0)
    norm_gain = jnp.clip(1.0 + 0.1 * jax.random.normal(arg_keys[5], (D,), jnp.float32), 0.5, 1.5)
    gate_logits = centred(arg_keys[6], (TOKENS, D), 2.0, 8.0, ((0, 32),))
    return {"queries": queries, "key_rows": key_rows, "values": values, "write_gate": write_gate, "ridge_diag": ridge_diag, "norm_gain": norm_gain, "gate_logits": gate_logits}


precise = lax.Precision.HIGHEST

def normalize(block):
    return block * lax.rsqrt(lax.optimization_barrier(jnp.sum(block * block, axis=-1, keepdims=True)) + 1e-06)

def one_head(inputs):
    query_n, key_n, value_f, gate_h, ridge_h = inputs
    count = TOKENS // TOK_DEV
    query_b = query_n.reshape(count, TOK_DEV, DH)
    key_b = key_n.reshape(count, TOK_DEV, DH)
    value_b = value_f.reshape(count, TOK_DEV, DH)
    gate_b = gate_h.reshape(count, TOK_DEV)
    causal = jnp.arange(TOK_DEV)[:, None] >= jnp.arange(TOK_DEV)[None, :]

    def step(carry, block):
        state_kk, state_vk = carry
        q_blk, k_blk, v_blk, g_blk = block
        weights = jnp.where(causal, g_blk[None, :], jnp.float32(0.0))

        def apply(direction):
            scores = jnp.dot(direction, k_blk.T, precision=precise)
            inner = jnp.dot(weights * scores, k_blk, precision=precise)
            return jnp.dot(direction, state_kk, precision=precise) + inner + ridge_h[None, :] * direction
        iterate = jnp.zeros_like(q_blk)
        residual = q_blk
        direction = q_blk
        norm_now = lax.optimization_barrier(jnp.sum(residual * residual, axis=-1, keepdims=True))
        for sweep in range(ITERS):
            image = apply(direction)
            alpha = norm_now / lax.optimization_barrier(jnp.sum(direction * image, axis=-1, keepdims=True))
            iterate = iterate + alpha * direction
            residual = residual - alpha * image
            norm_next = lax.optimization_barrier(jnp.sum(residual * residual, axis=-1, keepdims=True))
            direction = residual + norm_next / norm_now * direction
            norm_now = norm_next
        scores = jnp.dot(iterate, k_blk.T, precision=precise)
        result = jnp.dot(iterate, state_vk.T, precision=precise) + jnp.dot(weights * scores, v_blk, precision=precise)
        state_kk = state_kk + jnp.dot((k_blk * g_blk[:, None]).T, k_blk, precision=precise)
        state_vk = state_vk + jnp.dot((v_blk * g_blk[:, None]).T, k_blk, precision=precise)
        return ((state_kk, state_vk), result)
    empty_state = jnp.zeros((DH, DH), jnp.float32)
    unused, results = lax.scan(step, (empty_state, empty_state), (query_b, key_b, value_b, gate_b))
    return results.reshape(TOKENS, DH)

def reference(queries, key_rows, values, write_gate, ridge_diag, norm_gain, gate_logits):

    def split_heads(block):
        return block.astype(jnp.float32).reshape(TOKENS, HEADS, DH).transpose(1, 0, 2)
    query_n = normalize(split_heads(queries))
    key_n = normalize(split_heads(key_rows))
    value_f = split_heads(values)
    results = lax.map(one_head, (query_n, key_n, value_f, write_gate.T, ridge_diag))
    mesa_out = results.transpose(1, 0, 2).reshape(TOKENS, HEADS * DH).astype(jnp.bfloat16)
    wide_rows = lax.optimization_barrier(mesa_out).astype(jnp.float32)
    factor = lax.rsqrt(lax.optimization_barrier(jnp.mean(wide_rows * wide_rows, axis=-1, keepdims=True)) + 1e-06)
    gated = wide_rows * factor * norm_gain[None, :] * jax.nn.sigmoid(gate_logits.astype(jnp.float32))
    return gated.astype(jnp.bfloat16)
```

```python
import functools

import jax
import jax.numpy as jnp
from jax import lax
from jax.experimental import pallas as pl
from jax.experimental.pallas import tpu as pltpu
from jax.sharding import PartitionSpec as P

ITERS = 8
GROUP = 2
EPS = 1e-06

F32 = jnp.float32
BF16 = jnp.bfloat16
VMEM = pl.BlockSpec(memory_space=pltpu.VMEM)


def column(block, h):
    lane = lax.broadcasted_iota(jnp.int32, block.shape, 1)
    return jnp.sum(jnp.where(lane == h, block, 0.0), axis=1, keepdims=True)


def dot(a, b, dims=((1,), (0,))):
    return lax.dot_general(a, b, (dims, ((), ())), preferred_element_type=F32)


def states_kernel(width, k_ref, v_ref, gate_ref, kk_ref, vk_ref):
    heads = gate_ref.shape[1]
    half = width // 2
    row = lax.broadcasted_iota(jnp.int32, (half, width), 0)
    col = lax.broadcasted_iota(jnp.int32, (half, width), 1)
    eye = lax.broadcasted_iota(jnp.int32, (width, width), 0) == lax.broadcasted_iota(
        jnp.int32, (width, width), 1
    )
    diags = []
    for h in range(heads):
        cols = pl.ds(h * width, width)
        key = k_ref[:, cols]
        key_f = key.astype(F32)
        gate = gate_ref[:, h : h + 1]
        total = jnp.sum(key_f * key_f, axis=1, keepdims=True) + EPS
        scale = lax.rsqrt(total)
        wide = key_f * (gate * scale * scale)
        diags.append(jnp.sum(wide * key_f, axis=0, keepdims=True))
        val = (v_ref[:, cols].astype(F32) * (gate * scale)).astype(BF16)
        kk = dot(wide.astype(BF16), key, ((0,), (0,)))
        kk = jnp.where(eye, 0.0, kk)
        other = pltpu.roll(kk[half:], half, 1)
        kk_ref[h * half : (h + 1) * half] = jnp.where(row > col, other, kk[:half]).astype(BF16)
        vk_ref[h] = dot(val, key, ((0,), (0,))).astype(BF16)
    store_diag(kk_ref, heads * half, jnp.concatenate(diags, axis=0))


def store_diag(ref, at, diag):
    heads = diag.shape[0]
    high = diag.astype(BF16)
    ref[at : at + 2 * heads] = jnp.concatenate(
        [high, (diag - high.astype(F32)).astype(BF16)], axis=0
    )


def load_diag(ref, at):
    both = ref[at:].astype(F32)
    return both[: both.shape[0] // 2] + both[both.shape[0] // 2 :]


def join_kernel(step, last, place_ref, mine_ref, other_ref, before_ref, out_ref, diag_ref, *total):
    at = mine_ref.shape[0] - 2 * diag_ref.shape[0]
    later = ((place_ref[0] & step) != 0).astype(F32)
    other = other_ref[:at].astype(F32)
    other_diag = load_diag(other_ref, at)
    if step == 1:
        out_ref[...] = later * other
        diag_ref[...] = later * other_diag
    else:
        out_ref[...] = before_ref[0][...] + later * other
        diag_ref[...] = before_ref[1][...] + later * other_diag
    if not last:
        total[0][:at] = (mine_ref[:at].astype(F32) + other).astype(BF16)
        store_diag(total[0], at, load_diag(mine_ref, at) + other_diag)


def cg_kernel(width, q_ref, k_ref, gate_ref, ridge_ref, s_ref, x_ref, lhs, kt, wts, ridges, xs, rs, ps):
    toks = q_ref.shape[0]
    half = toks // 2
    first = pl.program_id(0) * GROUP
    row = lax.broadcasted_iota(jnp.int32, (half, half), 0)
    col = lax.broadcasted_iota(jnp.int32, (half, half), 1)
    norms = []
    for j in range(GROUP):
        cols = slice(j * width, (j + 1) * width)
        key = k_ref[:, cols]
        key_f = key.astype(F32)
        total = jnp.sum(key_f * key_f, axis=1, keepdims=True) + EPS
        weight = column(gate_ref[...], first + j) / total
        wts[j, :half, :half] = jnp.where(row <= col, weight[:half], 0.0)
        wts[j, :half, half:] = jnp.broadcast_to(weight[:half], (half, half))
        wts[j, half:, half:] = jnp.where(row <= col, weight[half:], 0.0)
        part = width // 2
        upper = s_ref[j * part : (j + 1) * part]
        turned = upper.T
        tri = upper[:, :part]
        tri_t = turned[:part]
        inner = row[:part, :part] < col[:part, :part]
        lhs[j, :toks] = key
        lhs[j, toks : toks + part] = jnp.concatenate(
            [jnp.where(inner, tri, tri_t), upper[:, part:]], axis=1
        ).astype(BF16)
        lhs[j, toks + part :] = jnp.concatenate(
            [turned[part:], jnp.where(inner, tri_t, tri)], axis=1
        ).astype(BF16)
        ridges[j] = jnp.broadcast_to(ridge_ref[pl.ds(first + j, 1), :], (width, width)).T
        kt[j] = key.T
        query = q_ref[:, cols].T.astype(F32)
        query = query * lax.rsqrt(jnp.sum(query * query, axis=0, keepdims=True) + EPS)
        xs[j] = jnp.zeros_like(query)
        rs[j] = query
        ps[j] = query
        norms.append(jnp.sum(query * query, axis=0, keepdims=True))

    def project(j):
        direction = ps[j]
        out = dot(lhs[j], direction.astype(BF16))
        ridge = jnp.concatenate([ridges[j]] * (toks // width), axis=1)
        return direction, out, out[toks:] + ridge * direction

    def step(_, norms):
        after = []
        for j in range(GROUP):
            direction, out, image = project(j)
            top = jnp.concatenate(
                [
                    (wts[j, :half, :half] * out[:half, :half]).astype(BF16),
                    (wts[j, :half, half:] * out[:half, half:]).astype(BF16),
                ],
                axis=1,
            )
            low = jnp.concatenate(
                [
                    jnp.zeros((half, half), BF16),
                    (wts[j, half:, half:] * out[half:toks, half:]).astype(BF16),
                ],
                axis=1,
            )
            image = image + dot(kt[j], jnp.concatenate([top, low], axis=0))
            alpha = norms[j] / jnp.sum(direction * image, axis=0, keepdims=True)
            xs[j] = xs[j] + alpha * direction
            residual = rs[j] - alpha * image
            rs[j] = residual
            following = jnp.sum(residual * residual, axis=0, keepdims=True)
            ps[j] = residual + (following / norms[j]) * direction
            after.append(following)
        return tuple(after)

    norms = lax.fori_loop(0, ITERS - 1, step, tuple(norms))
    for j in range(GROUP):
        direction, out, image = project(j)
        curve = jnp.sum(direction * image, axis=0, keepdims=True)
        score = out[:half]
        upper = jnp.sum(score[:, :half] * score[:, :half] * wts[j, :half, :half], axis=0, keepdims=True)
        lower = jnp.sum(score[:, half:] * score[:, half:] * wts[j, :half, half:], axis=0, keepdims=True)
        score = out[half:toks, half:]
        lower = lower + jnp.sum(score * score * wts[j, half:, half:], axis=0, keepdims=True)
        alpha = norms[j] / (curve + jnp.concatenate([upper, lower], axis=1))
        x_ref[j] = (xs[j] + alpha * direction).astype(BF16)


def read_kernel(width, spots, me_ref, x_ref, k_ref, v_ref, gate_ref, g_ref, *rest):
    outs, tmp = rest[:spots], rest[spots]
    toks = k_ref.shape[0]
    rows = toks // spots
    me = me_ref[0]
    keep = lax.broadcasted_iota(jnp.int32, (toks, toks), 0) >= lax.broadcasted_iota(
        jnp.int32, (toks, toks), 1
    )
    for h in range(gate_ref.shape[1]):
        cols = pl.ds(h * width, width)
        key = k_ref[:, cols]
        key_f = key.astype(F32)
        scale = lax.rsqrt(jnp.sum(key_f * key_f, axis=1, keepdims=True) + EPS)
        val = (v_ref[:, cols].astype(F32) * (gate_ref[:, h : h + 1] * scale)).astype(BF16)
        x = x_ref[h].T
        score = jnp.where(keep, dot(x, key, ((1,), (1,))), 0.0).astype(BF16)
        out = dot(x, g_ref[h].astype(BF16), ((1,), (1,))) + dot(score, val)
        tmp[:, cols] = out.astype(BF16)
    for k in range(spots):
        outs[k][...] = tmp[pl.ds(pl.multiple_of((me ^ k) * rows, rows), rows), :]


def norm_kernel(spots, me_ref, *refs):
    pieces, gain_ref, logit_ref, out_ref = refs[:spots], refs[spots], refs[spots + 1], refs[spots + 2]
    me = me_ref[0]
    wide = pieces[0].shape[1]
    total = 0.0
    for k in range(spots):
        piece = pieces[k][...].astype(F32)
        total = total + jnp.sum(piece * piece, axis=1, keepdims=True)
    factor = lax.rsqrt(total / (wide * spots) + EPS)
    for k in range(spots):
        cols = pl.ds(pl.multiple_of((me ^ k) * wide, wide), wide)
        piece = pieces[k][...].astype(F32) * factor
        gated = piece * gain_ref[:, cols] * jax.nn.sigmoid(logit_ref[:, cols].astype(F32))
        out_ref[:, cols] = gated.astype(BF16)


def exclusive_sum(local, axis, size):
    place = lax.axis_index(axis)
    total = local
    before = jnp.zeros(local.shape, F32)
    step = 1
    while step < size:
        other = lax.ppermute(total, axis, [(i, i ^ step) for i in range(size)]).astype(F32)
        before = before + jnp.where((place & step) != 0, other, 0.0)
        total = (total.astype(F32) + other).astype(BF16)
        step *= 2
    return before


def exclusive_join(packed, heads, size):
    place = lax.axis_index("seq").astype(jnp.int32).reshape(1)
    rows, width = packed.shape
    before = []
    step = 1
    while step < size:
        last = 2 * step >= size
        other = lax.ppermute(packed, "seq", [(i, i ^ step) for i in range(size)])
        shapes = [
            jax.ShapeDtypeStruct((rows - 2 * heads, width), F32),
            jax.ShapeDtypeStruct((heads, width), F32),
        ] + ([] if last else [jax.ShapeDtypeStruct((rows, width), BF16)])
        count = len(before)

        def body(*refs, step=step, last=last, count=count):
            join_kernel(step, last, refs[0], refs[1], refs[2], refs[3 : 3 + count], *refs[3 + count :])

        outs = pl.pallas_call(
            body,
            out_shape=shapes,
            in_specs=[pl.BlockSpec(memory_space=pltpu.SMEM)] + [VMEM] * (2 + count),
            out_specs=[VMEM] * len(shapes),
        )(place, packed, other, *before)
        before = outs[:2]
        packed = outs[-1]
        step *= 2
    return before


def shards(mesh, queries, key_rows, values, write_gate, ridge_diag, norm_gain, gate_logits):
    toks = queries.shape[0]
    heads = write_gate.shape[1]
    width = queries.shape[1] // heads
    spots = mesh.shape["head"]
    size = mesh.shape["seq"]
    rows = toks // spots
    me = lax.axis_index("head").astype(jnp.int32).reshape(1)

    kk, vk = pl.pallas_call(
        functools.partial(states_kernel, width),
        out_shape=[
            jax.ShapeDtypeStruct((heads * width // 2 + 2 * heads, width), BF16),
            jax.ShapeDtypeStruct((heads, width, width), BF16),
        ],
        in_specs=[VMEM] * 3,
        out_specs=[VMEM] * 2,
    )(key_rows, values, write_gate)
    prev_kk, diag = exclusive_join(kk, heads, size)
    prev_vk = exclusive_sum(vk, "seq", size)

    x = pl.pallas_call(
        functools.partial(cg_kernel, width),
        out_shape=jax.ShapeDtypeStruct((heads, width, toks), BF16),
        grid=(heads // GROUP,),
        in_specs=[
            pl.BlockSpec((toks, GROUP * width), lambda i: (0, i)),
            pl.BlockSpec((toks, GROUP * width), lambda i: (0, i)),
            pl.BlockSpec((toks, heads), lambda i: (0, 0)),
            pl.BlockSpec((heads, width), lambda i: (0, 0)),
            pl.BlockSpec((GROUP * width // 2, width), lambda i: (i, 0)),
        ],
        out_specs=pl.BlockSpec((GROUP, width, toks), lambda i: (i, 0, 0)),
        scratch_shapes=[
            pltpu.VMEM((GROUP, toks + width, width), BF16),
            pltpu.VMEM((GROUP, width, toks), BF16),
            pltpu.VMEM((GROUP, toks, toks), F32),
            pltpu.VMEM((GROUP, width, width), F32),
            pltpu.VMEM((GROUP, width, toks), F32),
            pltpu.VMEM((GROUP, width, toks), F32),
            pltpu.VMEM((GROUP, width, toks), F32),
        ],
    )(queries, key_rows, write_gate, ridge_diag + diag, prev_kk)

    pieces = pl.pallas_call(
        functools.partial(read_kernel, width, spots),
        out_shape=[jax.ShapeDtypeStruct((rows, heads * width), BF16)] * spots,
        in_specs=[pl.BlockSpec(memory_space=pltpu.SMEM)] + [VMEM] * 5,
        out_specs=[VMEM] * spots,
        scratch_shapes=[pltpu.VMEM((toks, heads * width), BF16)],
    )(me, x, key_rows, values, write_gate, prev_vk)
    arrived = [pieces[0]] + [
        lax.ppermute(pieces[k], "head", [(i, i ^ k) for i in range(spots)]) for k in range(1, spots)
    ]
    return pl.pallas_call(
        functools.partial(norm_kernel, spots),
        out_shape=jax.ShapeDtypeStruct((rows, spots * heads * width), BF16),
        in_specs=[pl.BlockSpec(memory_space=pltpu.SMEM)] + [VMEM] * (spots + 2),
        out_specs=VMEM,
    )(me, *arrived, norm_gain[None, :], gate_logits)


def solution(mesh):
    return jax.shard_map(
        functools.partial(shards, mesh),
        mesh=mesh,
        in_specs=(
            P("seq", "head"),
            P("seq", "head"),
            P("seq", "head"),
            P("seq", "head"),
            P("head", None),
            P(),
            P(("seq", "head"), None),
        ),
        out_specs=P(("seq", "head"), None),
        check_vma=False,
    )
```

```python
import functools

import jax
import jax.numpy as jnp
from jax import lax
from jax.experimental import pallas as pl
from jax.experimental.pallas import tpu as pltpu
from jax.sharding import PartitionSpec as P


ITERS = 8
EPS = 1e-06

F32 = jnp.float32
BF16 = jnp.bfloat16
VMEM = pl.BlockSpec(memory_space=pltpu.VMEM)
SMEM = pl.BlockSpec(memory_space=pltpu.SMEM)


def call(body, shapes, specs, scratch=(), mib=16, flops=0):
    single = not isinstance(shapes, list)
    return pl.pallas_call(
        body,
        out_shape=shapes,
        in_specs=specs,
        out_specs=VMEM if single else [VMEM] * len(shapes),
        scratch_shapes=list(scratch),
        compiler_params=pltpu.CompilerParams(vmem_limit_bytes=mib << 20),
        cost_estimate=pl.CostEstimate(flops=flops, bytes_accessed=1 << 20, transcendentals=0),
    )


def dot(a, b, dims=((1,), (0,))):
    return lax.dot_general(a, b, (dims, ((), ())), preferred_element_type=F32)


def square_sum(block, axis):
    return jnp.sum(block * block, axis=axis, keepdims=True)


def key_state_kernel(width, k_ref, gate_ref, kk_ref):
    heads = gate_ref.shape[0]
    half = width // 2
    row = lax.broadcasted_iota(jnp.int32, (half, width), 0)
    col = lax.broadcasted_iota(jnp.int32, (half, width), 1)
    gates = gate_ref[...].T
    diags = []
    for h in range(heads):
        key = k_ref[:, h * width : (h + 1) * width]
        key_f = key.astype(F32)
        wide = key_f * (gates[:, h : h + 1] / (square_sum(key_f, 1) + EPS))
        diags.append(jnp.sum(wide * key_f, axis=0, keepdims=True))
        kk = dot(wide.astype(BF16), key, ((0,), (0,)))
        other = pltpu.roll(kk[half:], half, 1)
        packed = jnp.where(row > col, other, jnp.where(row == col, 0.0, kk[:half]))
        kk_ref[h * half : (h + 1) * half] = packed.astype(BF16)
    store_diag(kk_ref, heads * half, jnp.concatenate(diags, axis=0))


def store_diag(ref, at, diag):
    heads = diag.shape[0]
    high = diag.astype(BF16)
    ref[at : at + 2 * heads] = jnp.concatenate(
        [high, (diag - high.astype(F32)).astype(BF16)], axis=0
    )


def load_diag(ref, at):
    both = ref[at:].astype(F32)
    heads = both.shape[0] // 2
    return both[:heads] + both[heads:]


def key_join_kernel(at, mine_ref, other_ref, total_ref):
    total_ref[:at] = (mine_ref[:at].astype(F32) + other_ref[:at].astype(F32)).astype(BF16)
    store_diag(total_ref, at, load_diag(mine_ref, at) + load_diag(other_ref, at))


def value_join_kernel(mine_ref, other_ref, total_ref):
    total_ref[...] = (mine_ref[...].astype(F32) + other_ref[...].astype(F32)).astype(BF16)


def value_state_kernel(width, k_ref, v_ref, gate_ref, val_ref, vk_ref):
    gates = gate_ref[...].T
    for h in range(gate_ref.shape[0]):
        cols = slice(h * width, (h + 1) * width)
        key = k_ref[:, cols]
        scale = lax.rsqrt(square_sum(key.astype(F32), 1) + EPS)
        val = (v_ref[:, cols].astype(F32) * (gates[:, h : h + 1] * scale)).astype(BF16)
        val_ref[:, cols] = val
        vk_ref[h] = dot(val, key, ((0,), (0,))).astype(BF16)


def prepare_kernel(width, q_ref, k_ref, gate_ref, kt_ref, qt_ref, wt_ref):
    heads, toks = gate_ref.shape
    half = toks // 2
    gates = gate_ref[...].T
    keep = lax.broadcasted_iota(jnp.int32, (half, half), 0) <= lax.broadcasted_iota(
        jnp.int32, (half, half), 1
    )
    for h in range(heads):
        cols = slice(h * width, (h + 1) * width)
        key = k_ref[:, cols]
        kt_ref[h] = key.T
        weight = gates[:, h : h + 1] / (square_sum(key.astype(F32), 1) + EPS)
        wt_ref[h, 0] = jnp.where(keep, weight[:half], 0.0)
        wt_ref[h, 1] = jnp.broadcast_to(weight[:half], (half, half))
        wt_ref[h, 2] = jnp.where(keep, weight[half:], 0.0)
        query = q_ref[:, cols].T.astype(F32)
        qt_ref[h] = query * lax.rsqrt(square_sum(query, 0) + EPS)


def gate_kernel(gain_ref, logit_ref, out_ref):
    out_ref[...] = gain_ref[...] * jax.nn.sigmoid(logit_ref[...].astype(F32))


def prefix(place_ref, refs, load):
    total = 0.0
    for k, ref in enumerate(refs):
        total = total + load(ref) * ((place_ref[0] >> k) & 1).astype(F32)
    return total


def cg_kernel(width, rounds, place_ref, k_ref, kt_ref, qt_ref, wt_ref, ridge_ref, *refs):
    totals = refs[:rounds]
    x_ref, lhs, ridges, rs, ps, xs = refs[rounds:]
    heads, _, toks = qt_ref.shape
    half = toks // 2
    part = width // 2
    inner = lax.broadcasted_iota(jnp.int32, (part, part), 0) < lax.broadcasted_iota(
        jnp.int32, (part, part), 1
    )
    ridge_t = (ridge_ref[...] + prefix(place_ref, totals, lambda ref: load_diag(ref, heads * part))).T
    norms = []
    for h in range(heads):
        rows = slice(h * part, (h + 1) * part)
        upper = prefix(place_ref, totals, lambda ref: ref[rows].astype(F32))
        turned = upper.T
        tri = upper[:, :part]
        tri_t = turned[:part]
        lhs[h, :toks] = k_ref[:, h * width : (h + 1) * width]
        lhs[h, toks : toks + part] = jnp.concatenate(
            [jnp.where(inner, tri, tri_t), upper[:, part:]], axis=1
        ).astype(BF16)
        lhs[h, toks + part :] = jnp.concatenate(
            [turned[part:], jnp.where(inner, tri_t, tri)], axis=1
        ).astype(BF16)
        ridges[h] = jnp.broadcast_to(ridge_t[:, h : h + 1], (width, width))
        query = qt_ref[h]
        xs[h] = jnp.zeros_like(query)
        rs[h] = query
        ps[h] = query
        norms.append(square_sum(query, 0))

    def project(h):
        direction = ps[h]
        out = dot(lhs[h], direction.astype(BF16))
        ridge = jnp.concatenate([ridges[h]] * (toks // width), axis=1)
        return direction, out, out[toks:] + ridge * direction

    def step(_, norms):
        after = []
        for h in range(heads):
            direction, out, image = project(h)
            top = jnp.concatenate(
                [
                    (wt_ref[h, 0] * out[:half, :half]).astype(BF16),
                    (wt_ref[h, 1] * out[:half, half:]).astype(BF16),
                ],
                axis=1,
            )
            low = jnp.concatenate(
                [
                    jnp.zeros((half, half), BF16),
                    (wt_ref[h, 2] * out[half:toks, half:]).astype(BF16),
                ],
                axis=1,
            )
            image = image + dot(kt_ref[h], jnp.concatenate([top, low], axis=0))
            alpha = norms[h] / jnp.sum(direction * image, axis=0, keepdims=True)
            xs[h] = xs[h] + alpha * direction
            residual = rs[h] - alpha * image
            rs[h] = residual
            following = square_sum(residual, 0)
            ps[h] = residual + (following / norms[h]) * direction
            after.append(following)
        return tuple(after)

    norms = lax.fori_loop(0, ITERS - 1, step, tuple(norms))
    for h in range(heads):
        direction, out, image = project(h)
        curve = jnp.sum(direction * image, axis=0, keepdims=True)
        score = out[:half]
        left = jnp.sum(score[:, :half] * score[:, :half] * wt_ref[h, 0], axis=0, keepdims=True)
        right = jnp.sum(score[:, half:] * score[:, half:] * wt_ref[h, 1], axis=0, keepdims=True)
        score = out[half:toks, half:]
        right = right + jnp.sum(score * score * wt_ref[h, 2], axis=0, keepdims=True)
        alpha = norms[h] / (curve + jnp.concatenate([left, right], axis=1))
        x_ref[:, h * width : (h + 1) * width] = (xs[h] + alpha * direction).astype(BF16).T


def read_kernel(width, spots, rounds, place_ref, me_ref, x_ref, k_ref, val_ref, *refs):
    totals, outs, tmp = refs[:rounds], refs[rounds : rounds + spots], refs[rounds + spots]
    toks = k_ref.shape[0]
    rows = toks // spots
    me = me_ref[0]
    keep = lax.broadcasted_iota(jnp.int32, (toks, toks), 0) >= lax.broadcasted_iota(
        jnp.int32, (toks, toks), 1
    )
    for h in range(k_ref.shape[1] // width):
        cols = slice(h * width, (h + 1) * width)
        x = x_ref[:, cols]
        state = prefix(place_ref, totals, lambda ref: ref[h].astype(F32)).astype(BF16)
        score = jnp.where(keep, dot(x, k_ref[:, cols], ((1,), (1,))), 0.0).astype(BF16)
        out = dot(x, state, ((1,), (1,))) + dot(score, val_ref[:, cols])
        tmp[:, cols] = out.astype(BF16)
    for k in range(spots):
        outs[k][...] = tmp[pl.ds(pl.multiple_of((me ^ k) * rows, rows), rows), :]


def norm_kernel(spots, me_ref, *refs):
    pieces, gate_ref, out_ref = refs[:spots], refs[spots], refs[spots + 1]
    me = me_ref[0]
    wide = pieces[0].shape[1]
    total = 0.0
    for k in range(spots):
        total = total + square_sum(pieces[k][...].astype(F32), 1)
    factor = lax.rsqrt(total / (wide * spots) + EPS)
    for k in range(spots):
        cols = pl.ds(pl.multiple_of((me ^ k) * wide, wide), wide)
        out_ref[:, cols] = (pieces[k][...].astype(F32) * factor * gate_ref[:, cols]).astype(BF16)


def swap(x, axis, size, step):
    return lax.ppermute(x, axis, [(i, i ^ step) for i in range(size)])


def shape(*dims, dtype=BF16):
    return jax.ShapeDtypeStruct(dims, dtype)


def shards(mesh, queries, key_rows, values, write_gate, ridge_diag, norm_gain, gate_logits):
    toks, cols = queries.shape
    heads = write_gate.shape[1]
    width = cols // heads
    spots = mesh.shape["head"]
    size = mesh.shape["seq"]
    rounds = size.bit_length() - 1
    rows = toks // spots
    me = lax.axis_index("head").astype(jnp.int32).reshape(1)
    place = lax.axis_index("seq").astype(jnp.int32).reshape(1)
    gates = write_gate.T
    packed = heads * width // 2 + 2 * heads
    work = 2 * toks * width * width * heads

    kk = call(
        functools.partial(key_state_kernel, width), shape(packed, width), [VMEM] * 2, flops=work
    )(key_rows, gates)
    vals, vk = call(
        functools.partial(value_state_kernel, width),
        [shape(toks, cols), shape(heads, width, width)],
        [VMEM] * 3,
        flops=work,
    )(key_rows, values, gates)
    kt, qt, wt = call(
        functools.partial(prepare_kernel, width),
        [
            shape(heads, width, toks),
            shape(heads, width, toks, dtype=F32),
            shape(heads, 3, toks // 2, toks // 2, dtype=F32),
        ],
        [VMEM] * 3,
        mib=24,
        flops=work,
    )(queries, key_rows, gates)
    gated = call(gate_kernel, shape(*gate_logits.shape, dtype=F32), [VMEM] * 2, flops=work)(
        norm_gain[None, :], gate_logits
    )

    key_in, value_in = [], []
    for k in range(rounds):
        key_in.append(swap(kk, "seq", size, 1 << k))
        if k + 1 < rounds:
            kk = call(
                functools.partial(key_join_kernel, packed - 2 * heads),
                shape(packed, width),
                [VMEM] * 2,
                mib=4,
            )(kk, key_in[-1])
    for k in range(rounds):
        value_in.append(swap(vk, "seq", size, 1 << k))
        if k + 1 < rounds:
            vk = call(value_join_kernel, shape(heads, width, width), [VMEM] * 2, mib=4)(
                vk, value_in[-1]
            )

    x = call(
        functools.partial(cg_kernel, width, rounds),
        shape(toks, cols),
        [SMEM] + [VMEM] * (5 + rounds),
        [
            pltpu.VMEM((heads, toks + width, width), BF16),
            pltpu.VMEM((heads, width, width), F32),
        ]
        + [pltpu.VMEM((heads, width, toks), F32)] * 3,
        mib=32,
        flops=20 * work,
    )(place, key_rows, kt, qt, wt, ridge_diag, *key_in)

    pieces = call(
        functools.partial(read_kernel, width, spots, rounds),
        [shape(rows, cols)] * spots,
        [SMEM] * 2 + [VMEM] * (3 + rounds),
        [pltpu.VMEM((toks, cols), BF16)],
        flops=work,
    )(place, me, x, key_rows, vals, *value_in)
    arrived = [pieces[0]] + [swap(pieces[k], "head", spots, k) for k in range(1, spots)]
    return call(
        functools.partial(norm_kernel, spots),
        shape(rows, spots * cols),
        [SMEM] + [VMEM] * (spots + 1),
        flops=work,
    )(me, *arrived, gated)


def solution(mesh):
    return jax.shard_map(
        functools.partial(shards, mesh),
        mesh=mesh,
        in_specs=(
            P("seq", "head"),
            P("seq", "head"),
            P("seq", "head"),
            P("seq", "head"),
            P("head", None),
            P(),
            P(("seq", "head"), None),
        ),
        out_specs=P(("seq", "head"), None),
        check_vma=False,
    )
```

```python
import functools

import jax
import jax.numpy as jnp
from jax import lax
from jax.experimental import pallas as pl
from jax.experimental.pallas import tpu as pltpu
from jax.sharding import PartitionSpec as P


ITERS = 8
EPS = 1e-06

F32 = jnp.float32
BF16 = jnp.bfloat16
VMEM = pl.BlockSpec(memory_space=pltpu.VMEM)


def call(body, shapes, specs, scratch=(), mib=4, flops=0):
    single = not isinstance(shapes, list)
    return pl.pallas_call(
        body,
        out_shape=shapes,
        in_specs=specs,
        out_specs=VMEM if single else [VMEM] * len(shapes),
        scratch_shapes=list(scratch),
        compiler_params=pltpu.CompilerParams(vmem_limit_bytes=mib << 20),
        cost_estimate=pl.CostEstimate(flops=flops, bytes_accessed=1 << 20, transcendentals=0),
    )


def dot(a, b, dims=((1,), (0,))):
    return lax.dot_general(a, b, (dims, ((), ())), preferred_element_type=F32)


def square_sum(block, axis):
    return jnp.sum(block * block, axis=axis, keepdims=True)


def key_state_kernel(width, k_ref, gate_ref, kk_ref):
    heads = gate_ref.shape[0]
    half = width // 2
    row = lax.broadcasted_iota(jnp.int32, (half, width), 0)
    col = lax.broadcasted_iota(jnp.int32, (half, width), 1)
    gates = gate_ref[...].T
    diags = []
    for h in range(heads):
        key = k_ref[:, h * width : (h + 1) * width]
        key_f = key.astype(F32)
        wide = key_f * (gates[:, h : h + 1] / (square_sum(key_f, 1) + EPS))
        diags.append(jnp.sum(wide * key_f, axis=0, keepdims=True))
        kk = dot(wide.astype(BF16), key, ((0,), (0,)))
        other = pltpu.roll(kk[half:], half, 1)
        packed = jnp.where(row > col, other, jnp.where(row == col, 0.0, kk[:half]))
        kk_ref[h * half : (h + 1) * half] = packed.astype(BF16)
    store_diag(kk_ref, heads * half, jnp.concatenate(diags, axis=0))


def store_diag(ref, at, diag):
    heads = diag.shape[0]
    high = diag.astype(BF16)
    ref[at : at + 2 * heads] = jnp.concatenate(
        [high, (diag - high.astype(F32)).astype(BF16)], axis=0
    )


def load_diag(ref, at):
    both = ref[at:].astype(F32)
    heads = both.shape[0] // 2
    return both[:heads] + both[heads:]


def key_join_kernel(at, mine_ref, other_ref, total_ref):
    total_ref[:at] = (mine_ref[:at].astype(F32) + other_ref[:at].astype(F32)).astype(BF16)
    store_diag(total_ref, at, load_diag(mine_ref, at) + load_diag(other_ref, at))


def value_join_kernel(mine_ref, other_ref, total_ref):
    total_ref[...] = (mine_ref[...].astype(F32) + other_ref[...].astype(F32)).astype(BF16)


def value_state_kernel(width, k_ref, v_ref, gate_ref, val_ref, vk_ref):
    gates = gate_ref[...].T
    for h in range(gate_ref.shape[0]):
        cols = slice(h * width, (h + 1) * width)
        key = k_ref[:, cols]
        scale = lax.rsqrt(square_sum(key.astype(F32), 1) + EPS)
        val = (v_ref[:, cols].astype(F32) * (gates[:, h : h + 1] * scale)).astype(BF16)
        val_ref[:, cols] = val
        vk_ref[h] = dot(val, key, ((0,), (0,))).astype(BF16)


def prepare_kernel(width, q_ref, k_ref, gate_ref, kt_ref, qt_ref, wt_ref):
    heads, toks = gate_ref.shape
    half = toks // 2
    gates = gate_ref[...].T
    keep = lax.broadcasted_iota(jnp.int32, (half, half), 0) <= lax.broadcasted_iota(
        jnp.int32, (half, half), 1
    )
    for h in range(heads):
        cols = slice(h * width, (h + 1) * width)
        key = k_ref[:, cols]
        kt_ref[h] = key.T
        weight = gates[:, h : h + 1] / (square_sum(key.astype(F32), 1) + EPS)
        wt_ref[h, 0] = jnp.where(keep, weight[:half], 0.0)
        wt_ref[h, 1] = jnp.broadcast_to(weight[:half], (half, half))
        wt_ref[h, 2] = jnp.where(keep, weight[half:], 0.0)
        query = q_ref[:, cols].T.astype(F32)
        qt_ref[h] = query * lax.rsqrt(square_sum(query, 0) + EPS)


def gate_kernel(gain_ref, logit_ref, out_ref):
    out_ref[...] = gain_ref[...] * jax.nn.sigmoid(logit_ref[...].astype(F32))


def prefix(refs, load):
    place = lax.axis_index("seq")
    total = 0.0
    for k, ref in enumerate(refs):
        total = total + load(ref) * ((place >> k) & 1).astype(F32)
    return total


def cg_kernel(width, rounds, k_ref, kt_ref, qt_ref, wt_ref, ridge_ref, *refs):
    totals = refs[:rounds]
    x_ref, lhs, ridges, rs, ps, xs = refs[rounds:]
    heads, _, toks = qt_ref.shape
    half = toks // 2
    part = width // 2
    inner = lax.broadcasted_iota(jnp.int32, (part, part), 0) < lax.broadcasted_iota(
        jnp.int32, (part, part), 1
    )
    ridge_t = (ridge_ref[...] + prefix(totals, lambda ref: load_diag(ref, heads * part))).T
    norms = []
    for h in range(heads):
        rows = slice(h * part, (h + 1) * part)
        upper = prefix(totals, lambda ref: ref[rows].astype(F32))
        turned = upper.T
        tri = upper[:, :part]
        tri_t = turned[:part]
        lhs[h, :toks] = k_ref[:, h * width : (h + 1) * width]
        lhs[h, toks : toks + part] = jnp.concatenate(
            [jnp.where(inner, tri, tri_t), upper[:, part:]], axis=1
        ).astype(BF16)
        lhs[h, toks + part :] = jnp.concatenate(
            [turned[part:], jnp.where(inner, tri_t, tri)], axis=1
        ).astype(BF16)
        ridges[h] = jnp.broadcast_to(ridge_t[:, h : h + 1], (width, width))
        query = qt_ref[h]
        xs[h] = jnp.zeros_like(query)
        rs[h] = query
        ps[h] = query
        norms.append(square_sum(query, 0))

    def project(h):
        direction = ps[h]
        out = dot(lhs[h], direction.astype(BF16))
        ridge = jnp.concatenate([ridges[h]] * (toks // width), axis=1)
        return direction, out, out[toks:] + ridge * direction

    def step(_, norms):
        after = []
        for h in range(heads):
            direction, out, image = project(h)
            top = jnp.concatenate(
                [
                    (wt_ref[h, 0] * out[:half, :half]).astype(BF16),
                    (wt_ref[h, 1] * out[:half, half:]).astype(BF16),
                ],
                axis=1,
            )
            low = jnp.concatenate(
                [
                    jnp.zeros((half, half), BF16),
                    (wt_ref[h, 2] * out[half:toks, half:]).astype(BF16),
                ],
                axis=1,
            )
            image = image + dot(kt_ref[h], jnp.concatenate([top, low], axis=0))
            alpha = norms[h] / jnp.sum(direction * image, axis=0, keepdims=True)
            xs[h] = xs[h] + alpha * direction
            residual = rs[h] - alpha * image
            rs[h] = residual
            following = square_sum(residual, 0)
            ps[h] = residual + (following / norms[h]) * direction
            after.append(following)
        return tuple(after)

    norms = lax.fori_loop(0, ITERS - 1, step, tuple(norms))
    for h in range(heads):
        direction, out, image = project(h)
        curve = jnp.sum(direction * image, axis=0, keepdims=True)
        score = out[:half]
        left = jnp.sum(score[:, :half] * score[:, :half] * wt_ref[h, 0], axis=0, keepdims=True)
        right = jnp.sum(score[:, half:] * score[:, half:] * wt_ref[h, 1], axis=0, keepdims=True)
        score = out[half:toks, half:]
        right = right + jnp.sum(score * score * wt_ref[h, 2], axis=0, keepdims=True)
        alpha = norms[h] / (curve + jnp.concatenate([left, right], axis=1))
        x_ref[:, h * width : (h + 1) * width] = (xs[h] + alpha * direction).astype(BF16).T


def read_kernel(width, spots, rounds, x_ref, k_ref, val_ref, *refs):
    totals, outs, tmp = refs[:rounds], refs[rounds : rounds + spots], refs[rounds + spots]
    toks = k_ref.shape[0]
    rows = toks // spots
    me = lax.axis_index("head")
    keep = lax.broadcasted_iota(jnp.int32, (toks, toks), 0) >= lax.broadcasted_iota(
        jnp.int32, (toks, toks), 1
    )
    for h in range(k_ref.shape[1] // width):
        cols = slice(h * width, (h + 1) * width)
        x = x_ref[:, cols]
        state = prefix(totals, lambda ref: ref[h].astype(F32)).astype(BF16)
        score = jnp.where(keep, dot(x, k_ref[:, cols], ((1,), (1,))), 0.0).astype(BF16)
        out = dot(x, state, ((1,), (1,))) + dot(score, val_ref[:, cols])
        tmp[:, cols] = out.astype(BF16)
    for k in range(spots):
        outs[k][...] = tmp[pl.ds(pl.multiple_of((me ^ k) * rows, rows), rows), :]


def norm_kernel(spots, *refs):
    pieces, gate_ref, out_ref = refs[:spots], refs[spots], refs[spots + 1]
    me = lax.axis_index("head")
    wide = pieces[0].shape[1]
    total = 0.0
    for k in range(spots):
        total = total + square_sum(pieces[k][...].astype(F32), 1)
    factor = lax.rsqrt(total / (wide * spots) + EPS)
    for k in range(spots):
        cols = pl.ds(pl.multiple_of((me ^ k) * wide, wide), wide)
        out_ref[:, cols] = (pieces[k][...].astype(F32) * factor * gate_ref[:, cols]).astype(BF16)


def swap(x, axis, size, step):
    return lax.ppermute(x, axis, [(i, i ^ step) for i in range(size)])


def shape(*dims, dtype=BF16):
    return jax.ShapeDtypeStruct(dims, dtype)


def shards(mesh, queries, key_rows, values, write_gate, ridge_diag, norm_gain, gate_logits):
    toks, cols = queries.shape
    heads = write_gate.shape[1]
    width = cols // heads
    spots = mesh.shape["head"]
    size = mesh.shape["seq"]
    rounds = size.bit_length() - 1
    rows = toks // spots
    gates = write_gate.T
    packed = heads * width // 2 + 2 * heads
    work = 2 * toks * width * width * heads

    kk = call(
        functools.partial(key_state_kernel, width), shape(packed, width), [VMEM] * 2, flops=work
    )(key_rows, gates)
    vals, vk = call(
        functools.partial(value_state_kernel, width),
        [shape(toks, cols), shape(heads, width, width)],
        [VMEM] * 3,
        flops=work,
    )(key_rows, values, gates)
    kt, qt, wt = call(
        functools.partial(prepare_kernel, width),
        [
            shape(heads, width, toks),
            shape(heads, width, toks, dtype=F32),
            shape(heads, 3, toks // 2, toks // 2, dtype=F32),
        ],
        [VMEM] * 3,
        mib=4,
        flops=work,
    )(queries, key_rows, gates)
    gated = call(gate_kernel, shape(*gate_logits.shape, dtype=F32), [VMEM] * 2, flops=work)(
        norm_gain[None, :], gate_logits
    )

    key_in, value_in = [], []
    for k in range(rounds):
        key_in.append(swap(kk, "seq", size, 1 << k))
        if k + 1 < rounds:
            kk = call(
                functools.partial(key_join_kernel, packed - 2 * heads),
                shape(packed, width),
                [VMEM] * 2,
                mib=4,
            )(kk, key_in[-1])
    for k in range(rounds):
        value_in.append(swap(vk, "seq", size, 1 << k))
        if k + 1 < rounds:
            vk = call(value_join_kernel, shape(heads, width, width), [VMEM] * 2, mib=4)(
                vk, value_in[-1]
            )

    x = call(
        functools.partial(cg_kernel, width, rounds),
        shape(toks, cols),
        [VMEM] * (5 + rounds),
        [
            pltpu.VMEM((heads, toks + width, width), BF16),
            pltpu.VMEM((heads, width, width), F32),
        ]
        + [pltpu.VMEM((heads, width, toks), F32)] * 3,
        mib=8,
        flops=20 * work,
    )(key_rows, kt, qt, wt, ridge_diag, *key_in)

    pieces = call(
        functools.partial(read_kernel, width, spots, rounds),
        [shape(rows, cols)] * spots,
        [VMEM] * (3 + rounds),
        [pltpu.VMEM((toks, cols), BF16)],
        flops=work,
    )(x, key_rows, vals, *value_in)
    arrived = [pieces[0]] + [swap(pieces[k], "head", spots, k) for k in range(1, spots)]
    return call(
        functools.partial(norm_kernel, spots),
        shape(rows, spots * cols),
        [VMEM] * (spots + 1),
        flops=work,
    )(*arrived, gated)


def solution(mesh):
    return jax.shard_map(
        functools.partial(shards, mesh),
        mesh=mesh,
        in_specs=(
            P("seq", "head"),
            P("seq", "head"),
            P("seq", "head"),
            P("seq", "head"),
            P("head", None),
            P(),
            P(("seq", "head"), None),
        ),
        out_specs=P(("seq", "head"), None),
        check_vma=False,
    )
```

```python
import functools

import jax
import jax.numpy as jnp
from jax import lax
from jax.experimental import pallas as pl
from jax.experimental.pallas import tpu as pltpu
from jax.sharding import PartitionSpec as P


ITERS = 8
FIRST = 4
EPS = 1e-06

F32 = jnp.float32
BF16 = jnp.bfloat16
VMEM = pl.BlockSpec(memory_space=pltpu.VMEM)


def call(body, shapes, specs, scratch=(), mib=4, flops=0):
    single = not isinstance(shapes, list)
    return pl.pallas_call(
        body,
        out_shape=shapes,
        in_specs=specs,
        out_specs=VMEM if single else [VMEM] * len(shapes),
        scratch_shapes=list(scratch),
        compiler_params=pltpu.CompilerParams(vmem_limit_bytes=mib << 20),
        cost_estimate=pl.CostEstimate(flops=flops, bytes_accessed=1 << 20, transcendentals=0),
    )


def dot(a, b, dims=((1,), (0,))):
    return lax.dot_general(a, b, (dims, ((), ())), preferred_element_type=F32)


def square_sum(block, axis):
    return jnp.sum(block * block, axis=axis, keepdims=True)


def key_state_kernel(width, k_hbm, gate_hbm, kk_ref, kt_ref, k_ref, gate_ref, sems):
    heads = gate_ref.shape[0]
    half = width // 2
    loads = [pltpu.make_async_copy(gate_hbm, gate_ref, sems.at[heads])]
    for h in range(heads):
        cols = slice(h * width, (h + 1) * width)
        loads.append(pltpu.make_async_copy(k_hbm.at[:, cols], k_ref.at[:, cols], sems.at[h]))
    for load in loads:
        load.start()
    row = lax.broadcasted_iota(jnp.int32, (half, width), 0)
    col = lax.broadcasted_iota(jnp.int32, (half, width), 1)
    loads[0].wait()
    diags = []
    for h in range(heads):
        loads[1 + h].wait()
        key = k_ref[:, h * width : (h + 1) * width]
        turned = key.T
        kt_ref[h] = turned
        turned = turned.astype(F32)
        wide = turned * (gate_ref[h : h + 1] / (square_sum(turned, 0) + EPS))
        kk = dot(wide.astype(BF16), key)
        diag = jnp.where(row == col, kk[:half], jnp.where(row + half == col, kk[half:], 0.0))
        diags.append(jnp.sum(diag, axis=0, keepdims=True))
        other = pltpu.roll(kk[half:], half, 1)
        packed = jnp.where(row > col, other, jnp.where(row == col, 0.0, kk[:half]))
        kk_ref[h * half : (h + 1) * half] = packed.astype(BF16)
    store_diag(kk_ref, heads * half, jnp.concatenate(diags, axis=0))


def store_diag(ref, at, diag):
    heads = diag.shape[0]
    high = diag.astype(BF16)
    ref[at : at + 2 * heads] = jnp.concatenate(
        [high, (diag - high.astype(F32)).astype(BF16)], axis=0
    )


def load_diag(ref, at):
    both = ref[at:].astype(F32)
    heads = both.shape[0] // 2
    return both[:heads] + both[heads:]


def key_join_kernel(at, mine_ref, other_ref, total_ref):
    total_ref[:at] = (mine_ref[:at].astype(F32) + other_ref[:at].astype(F32)).astype(BF16)
    store_diag(total_ref, at, load_diag(mine_ref, at) + load_diag(other_ref, at))


def value_fold_kernel(mine_ref, other_ref, total_ref):
    count = total_ref.shape[0]
    part = pl.ds((lax.axis_index("seq") & 1) * count, count)
    total_ref[...] = (mine_ref[part].astype(F32) + other_ref[part].astype(F32)).astype(BF16)


def value_join_kernel(mine_ref, other_ref, total_ref):
    total_ref[...] = (mine_ref[...].astype(F32) + other_ref[...].astype(F32)).astype(BF16)


def value_prefix_kernel(*refs):
    refs[-1][...] = prefix(refs[:-1], lambda ref: ref[...].astype(F32), 1).astype(BF16)


def value_state_kernel(width, k_ref, v_ref, gate_ref, val_ref, vk_ref):
    gates = gate_ref[...].T
    for h in range(gate_ref.shape[0]):
        cols = slice(h * width, (h + 1) * width)
        key = k_ref[:, cols]
        scale = lax.rsqrt(square_sum(key.astype(F32), 1) + EPS)
        val = (v_ref[:, cols].astype(F32) * (gates[:, h : h + 1] * scale)).astype(BF16)
        val_ref[:, cols] = val
        vk_ref[h] = dot(val, key, ((0,), (0,))).astype(BF16)


def prepare_kernel(width, q_ref, k_ref, gate_ref, qt_ref, wt_ref):
    heads, toks = gate_ref.shape
    half = toks // 2
    gates = gate_ref[...].T
    keep = lax.broadcasted_iota(jnp.int32, (half, half), 0) <= lax.broadcasted_iota(
        jnp.int32, (half, half), 1
    )
    for h in range(heads):
        cols = slice(h * width, (h + 1) * width)
        key = k_ref[:, cols]
        weight = gates[:, h : h + 1] / (square_sum(key.astype(F32), 1) + EPS)
        wt_ref[h, 0] = jnp.where(keep, weight[:half], 0.0)
        wt_ref[h, 1] = jnp.broadcast_to(weight[:half], (half, half))
        wt_ref[h, 2] = jnp.where(keep, weight[half:], 0.0)
        query = q_ref[:, cols].T.astype(F32)
        qt_ref[h] = query * lax.rsqrt(square_sum(query, 0) + EPS)


def gate_kernel(gain_ref, logit_ref, out_ref):
    out_ref[...] = gain_ref[...] * jax.nn.sigmoid(logit_ref[...].astype(F32))


def prefix(refs, load, first=0):
    place = lax.axis_index("seq")
    total = 0.0
    for k, ref in enumerate(refs):
        total = total + load(ref) * ((place >> (first + k)) & 1).astype(F32)
    return total


def project(lhs, ridges, ps, h):
    toks = ps.shape[2]
    direction = ps[h]
    out = dot(lhs[h], direction.astype(BF16))
    ridge = jnp.concatenate([ridges[h]] * (toks // ridges.shape[2]), axis=1)
    return direction, out, out[toks:] + ridge * direction


def sweep(kt_ref, wt_ref, lhs, ridges, old, new, norms):
    half = old[0].shape[2] // 2
    after = []
    for h in range(kt_ref.shape[0]):
        direction, out, image = project(lhs, ridges, old[1], h)
        top = jnp.concatenate(
            [
                (wt_ref[h, 0] * out[:half, :half]).astype(BF16),
                (wt_ref[h, 1] * out[:half, half:]).astype(BF16),
            ],
            axis=1,
        )
        low = jnp.concatenate(
            [
                jnp.zeros((half, half), BF16),
                (wt_ref[h, 2] * out[half : 2 * half, half:]).astype(BF16),
            ],
            axis=1,
        )
        image = image + dot(kt_ref[h], jnp.concatenate([top, low], axis=0))
        alpha = norms[h] / jnp.sum(direction * image, axis=0, keepdims=True)
        residual = old[0][h] - alpha * image
        new[0][h] = residual
        following = square_sum(residual, 0)
        new[1][h] = residual + (following / norms[h]) * direction
        step = alpha * direction
        new[2][h] = step if old[2] is None else old[2][h] + step
        after.append(following)
    return tuple(after)


def cg_first_kernel(width, rounds, sweeps, k_ref, kt_ref, qt_ref, wt_ref, ridge_ref, *refs):
    totals = refs[:rounds]
    lhs, ridges, norm_ref, *state = refs[rounds:]
    heads, _, toks = qt_ref.shape
    part = width // 2
    inner = lax.broadcasted_iota(jnp.int32, (part, part), 0) < lax.broadcasted_iota(
        jnp.int32, (part, part), 1
    )
    ridge_t = (ridge_ref[...] + prefix(totals, lambda ref: load_diag(ref, heads * part))).T
    norms = []
    for h in range(heads):
        rows = slice(h * part, (h + 1) * part)
        upper = prefix(totals, lambda ref: ref[rows].astype(F32))
        turned = upper.T
        tri = upper[:, :part]
        tri_t = turned[:part]
        lhs[h, :toks] = k_ref[:, h * width : (h + 1) * width]
        lhs[h, toks : toks + part] = jnp.concatenate(
            [jnp.where(inner, tri, tri_t), upper[:, part:]], axis=1
        ).astype(BF16)
        lhs[h, toks + part :] = jnp.concatenate(
            [turned[part:], jnp.where(inner, tri_t, tri)], axis=1
        ).astype(BF16)
        ridges[h] = jnp.broadcast_to(ridge_t[:, h : h + 1], (width, width))
        norms.append(square_sum(qt_ref[h], 0))
    fixed = (kt_ref, wt_ref, lhs, ridges)
    norms = sweep(*fixed, (qt_ref, qt_ref, None), state, norms)
    norms = lax.fori_loop(1, sweeps, lambda _, now: sweep(*fixed, state, state, now), norms)
    norm_ref[...] = jnp.concatenate(norms, axis=0)


def cg_last_kernel(width, sweeps, kt_ref, wt_ref, lhs, ridges, norm_ref, *refs):
    given, x_ref, state = refs[:3], refs[3], refs[4:]
    heads = kt_ref.shape[0]
    half = wt_ref.shape[2]
    fixed = (kt_ref, wt_ref, lhs, ridges)
    norms = tuple(norm_ref[h : h + 1] for h in range(heads))
    norms = sweep(*fixed, given, state, norms)
    norms = lax.fori_loop(1, sweeps, lambda _, now: sweep(*fixed, state, state, now), norms)
    for h in range(heads):
        direction, out, image = project(lhs, ridges, state[1], h)
        curve = jnp.sum(direction * image, axis=0, keepdims=True)
        score = out[:half]
        left = jnp.sum(score[:, :half] * score[:, :half] * wt_ref[h, 0], axis=0, keepdims=True)
        right = jnp.sum(score[:, half:] * score[:, half:] * wt_ref[h, 1], axis=0, keepdims=True)
        score = out[half : 2 * half, half:]
        right = right + jnp.sum(score * score * wt_ref[h, 2], axis=0, keepdims=True)
        alpha = norms[h] / (curve + jnp.concatenate([left, right], axis=1))
        x = state[2][h] + alpha * direction
        x_ref[:, h * width : (h + 1) * width] = x.astype(BF16).T


def read_kernel(width, spots, x_ref, k_ref, val_ref, near_ref, own_ref, far_ref, *refs):
    outs, tmp = refs[:spots], refs[spots]
    count = own_ref.shape[0]
    later = lax.axis_index("seq") & 1
    toks = k_ref.shape[0]
    rows = toks // spots
    me = lax.axis_index("head")
    keep = lax.broadcasted_iota(jnp.int32, (toks, toks), 0) >= lax.broadcasted_iota(
        jnp.int32, (toks, toks), 1
    )
    for h in range(k_ref.shape[1] // width):
        cols = slice(h * width, (h + 1) * width)
        x = x_ref[:, cols]
        state = jnp.where(later == h // count, own_ref[h % count], far_ref[h % count])
        near = near_ref[h].astype(F32) * later.astype(F32)
        state = (state.astype(F32) + near).astype(BF16)
        score = jnp.where(keep, dot(x, k_ref[:, cols], ((1,), (1,))), 0.0).astype(BF16)
        out = dot(x, state, ((1,), (1,))) + dot(score, val_ref[:, cols])
        tmp[:, cols] = out.astype(BF16)
    for k in range(spots):
        outs[k][...] = tmp[pl.ds(pl.multiple_of((me ^ k) * rows, rows), rows), :]


def norm_kernel(spots, *refs):
    pieces, gate_ref, out_ref = refs[:spots], refs[spots], refs[spots + 1]
    me = lax.axis_index("head")
    wide = pieces[0].shape[1]
    total = 0.0
    for k in range(spots):
        total = total + square_sum(pieces[k][...].astype(F32), 1)
    factor = lax.rsqrt(total / (wide * spots) + EPS)
    for k in range(spots):
        cols = pl.ds(pl.multiple_of((me ^ k) * wide, wide), wide)
        out_ref[:, cols] = (pieces[k][...].astype(F32) * factor * gate_ref[:, cols]).astype(BF16)


def swap(x, axis, size, step):
    return lax.ppermute(x, axis, [(i, i ^ step) for i in range(size)])


def shape(*dims, dtype=BF16):
    return jax.ShapeDtypeStruct(dims, dtype)


def shards(mesh, queries, key_rows, values, write_gate, ridge_diag, norm_gain, gate_logits):
    toks, cols = queries.shape
    heads = write_gate.shape[1]
    width = cols // heads
    spots = mesh.shape["head"]
    size = mesh.shape["seq"]
    rounds = size.bit_length() - 1
    rows = toks // spots
    gates = write_gate.T
    packed = heads * width // 2 + 2 * heads
    work = 2 * toks * width * width * heads

    kk, kt = call(
        functools.partial(key_state_kernel, width),
        [shape(packed, width), shape(heads, width, toks)],
        [pl.BlockSpec(memory_space=pltpu.MemorySpace.HBM)] * 2,
        [
            pltpu.VMEM((toks, cols), BF16),
            pltpu.VMEM((heads, toks), F32),
            pltpu.SemaphoreType.DMA((heads + 1,)),
        ],
        flops=work,
    )(key_rows, gates)
    vals, vk = call(
        functools.partial(value_state_kernel, width),
        [shape(toks, cols), shape(heads, width, width)],
        [VMEM] * 3,
        flops=work,
    )(key_rows, values, gates)
    qt, wt = call(
        functools.partial(prepare_kernel, width),
        [
            shape(heads, width, toks, dtype=F32),
            shape(heads, 3, toks // 2, toks // 2, dtype=F32),
        ],
        [VMEM] * 3,
        mib=4,
        flops=work,
    )(queries, key_rows, gates)
    gated = call(gate_kernel, shape(*gate_logits.shape, dtype=F32), [VMEM] * 2, flops=work)(
        norm_gain[None, :], gate_logits
    )

    key_in, value_in = [], []
    for k in range(rounds):
        key_in.append(swap(kk, "seq", size, 1 << k))
        if k + 1 < rounds:
            kk = call(
                functools.partial(key_join_kernel, packed - 2 * heads),
                shape(packed, width),
                [VMEM] * 2,
                mib=4,
            )(kk, key_in[-1])
    near = swap(vk, "seq", size, 1)
    vk = call(value_fold_kernel, shape(heads // 2, width, width), [VMEM] * 2)(vk, near)
    for k in range(1, rounds):
        value_in.append(swap(vk, "seq", size, 1 << k))
        if k + 1 < rounds:
            vk = call(value_join_kernel, shape(*vk.shape), [VMEM] * 2)(vk, value_in[-1])
    own = call(value_prefix_kernel, shape(*vk.shape), [VMEM] * (rounds - 1))(*value_in)
    far = swap(own, "seq", size, 1)

    lhs, ridges, norms, *state = call(
        functools.partial(cg_first_kernel, width, rounds, FIRST),
        [
            shape(heads, toks + width, width),
            shape(heads, width, width, dtype=F32),
            shape(heads, toks, dtype=F32),
        ]
        + [shape(heads, width, toks, dtype=F32)] * 3,
        [VMEM] * (5 + rounds),
        mib=4,
        flops=10 * work,
    )(key_rows, kt, qt, wt, ridge_diag, *key_in)
    x = call(
        functools.partial(cg_last_kernel, width, ITERS - 1 - FIRST),
        shape(toks, cols),
        [VMEM] * 8,
        [pltpu.VMEM((heads, width, toks), F32)] * 3,
        mib=8,
        flops=10 * work,
    )(kt, wt, lhs, ridges, norms, *state)

    pieces = call(
        functools.partial(read_kernel, width, spots),
        [shape(rows, cols)] * spots,
        [VMEM] * 6,
        [pltpu.VMEM((toks, cols), BF16)],
        flops=work,
    )(x, key_rows, vals, near, own, far)
    arrived = [pieces[0]] + [swap(pieces[k], "head", spots, k) for k in range(1, spots)]
    return call(
        functools.partial(norm_kernel, spots),
        shape(rows, spots * cols),
        [VMEM] * (spots + 1),
        flops=work,
    )(*arrived, gated)


def solution(mesh):
    return jax.shard_map(
        functools.partial(shards, mesh),
        mesh=mesh,
        in_specs=(
            P("seq", "head"),
            P("seq", "head"),
            P("seq", "head"),
            P("seq", "head"),
            P("head", None),
            P(),
            P(("seq", "head"), None),
        ),
        out_specs=P(("seq", "head"), None),
        check_vma=False,
    )
```

```python
import functools

import jax
import jax.numpy as jnp
from jax import lax
from jax.experimental import pallas as pl
from jax.experimental.pallas import tpu as pltpu
from jax.sharding import PartitionSpec as P


ITERS = 8
FIRST = 4
EPS = 1e-06

F32 = jnp.float32
BF16 = jnp.bfloat16
VMEM = pl.BlockSpec(memory_space=pltpu.VMEM)


def call(body, shapes, specs, scratch=(), mib=4, flops=0):
    single = not isinstance(shapes, list)
    return pl.pallas_call(
        body,
        out_shape=shapes,
        in_specs=specs,
        out_specs=VMEM if single else [VMEM] * len(shapes),
        scratch_shapes=list(scratch),
        compiler_params=pltpu.CompilerParams(vmem_limit_bytes=mib << 20),
        cost_estimate=pl.CostEstimate(flops=flops, bytes_accessed=1 << 20, transcendentals=0),
    )


def dot(a, b, dims=((1,), (0,))):
    return lax.dot_general(a, b, (dims, ((), ())), preferred_element_type=F32)


def square_sum(block, axis):
    return jnp.sum(block * block, axis=axis, keepdims=True)


def key_state_kernel(width, k_hbm, v_hbm, gate_hbm, kk_ref, kt_ref, k_ref, v_ref, scale_ref, gate_ref, sems):
    heads = gate_ref.shape[0]
    half = width // 2
    loads = [pltpu.make_async_copy(gate_hbm, gate_ref, sems.at[heads])]
    for h in range(heads):
        cols = slice(h * width, (h + 1) * width)
        loads.append(pltpu.make_async_copy(k_hbm.at[:, cols], k_ref.at[:, cols], sems.at[h]))
    loads.append(pltpu.make_async_copy(v_hbm, v_ref, sems.at[heads + 1]))
    for load in loads:
        load.start()
    row = lax.broadcasted_iota(jnp.int32, (half, width), 0)
    col = lax.broadcasted_iota(jnp.int32, (half, width), 1)
    loads[0].wait()
    diags = []
    for h in range(heads):
        loads[1 + h].wait()
        key = k_ref[:, h * width : (h + 1) * width]
        turned = key.T.astype(F32)
        total = square_sum(turned, 0) + EPS
        scale_ref[h : h + 1] = gate_ref[h : h + 1] * lax.rsqrt(total)
        wide = (turned * (gate_ref[h : h + 1] / total)).astype(BF16)
        kt_ref[h] = wide
        kk = dot(wide, key)
        diag = jnp.where(row == col, kk[:half], jnp.where(row + half == col, kk[half:], 0.0))
        diags.append(jnp.sum(diag, axis=0, keepdims=True))
        other = pltpu.roll(kk[half:], half, 1)
        packed = jnp.where(row > col, other, jnp.where(row == col, 0.0, kk[:half]))
        kk_ref[h * half : (h + 1) * half] = packed.astype(BF16)
    store_diag(kk_ref, heads * half, jnp.concatenate(diags, axis=0))
    loads[-1].wait()


def store_diag(ref, at, diag):
    heads = diag.shape[0]
    high = diag.astype(BF16)
    ref[at : at + 2 * heads] = jnp.concatenate(
        [high, (diag - high.astype(F32)).astype(BF16)], axis=0
    )


def load_diag(ref, at):
    both = ref[at:].astype(F32)
    heads = both.shape[0] // 2
    return both[:heads] + both[heads:]


def key_join_kernel(at, mine_ref, other_ref, total_ref):
    total_ref[:at] = (mine_ref[:at].astype(F32) + other_ref[:at].astype(F32)).astype(BF16)
    store_diag(total_ref, at, load_diag(mine_ref, at) + load_diag(other_ref, at))


def value_fold_kernel(mine_ref, other_ref, total_ref):
    count = total_ref.shape[0]
    part = pl.ds((lax.axis_index("seq") & 1) * count, count)
    total_ref[...] = (mine_ref[part].astype(F32) + other_ref[part].astype(F32)).astype(BF16)


def value_join_kernel(mine_ref, other_ref, total_ref):
    total_ref[...] = (mine_ref[...].astype(F32) + other_ref[...].astype(F32)).astype(BF16)


def value_prefix_kernel(*refs):
    refs[-1][...] = prefix(refs[:-1], lambda ref: ref[...].astype(F32), 1).astype(BF16)


def value_state_kernel(width, k_ref, v_ref, scale_ref, val_ref, vk_ref):
    scales = scale_ref[...].T
    for h in range(scale_ref.shape[0]):
        cols = slice(h * width, (h + 1) * width)
        val = (v_ref[:, cols].astype(F32) * scales[:, h : h + 1]).astype(BF16)
        val_ref[:, cols] = val
        vk_ref[h] = dot(val, k_ref[:, cols], ((0,), (0,))).astype(BF16)


def prepare_kernel(width, q_ref, qt_ref):
    for h in range(qt_ref.shape[0]):
        query = q_ref[:, h * width : (h + 1) * width].T.astype(F32)
        qt_ref[h] = query * lax.rsqrt(square_sum(query, 0) + EPS)


def gate_kernel(gain_ref, logit_ref, out_ref):
    out_ref[...] = gain_ref[...] * jax.nn.sigmoid(logit_ref[...].astype(F32))


def prefix(refs, load, first=0):
    place = lax.axis_index("seq")
    total = 0.0
    for k, ref in enumerate(refs):
        total = total + load(ref) * ((place >> (first + k)) & 1).astype(F32)
    return total


def operator(k_ref, lhs, directions, h):
    _, width, toks = directions.shape
    half = toks // 2
    low = directions[h].astype(BF16)
    score = dot(k_ref[:, h * width : (h + 1) * width], low).astype(BF16)
    keep = lax.broadcasted_iota(jnp.int32, (half, half), 0) <= lax.broadcasted_iota(
        jnp.int32, (half, half), 1
    )
    none = jnp.zeros((half, half), BF16)
    upper = jnp.concatenate([jnp.where(keep, score[:half, :half], none), score[:half, half:]], axis=1)
    lower = jnp.concatenate([none, jnp.where(keep, score[half:, half:], none)], axis=1)
    return dot(lhs[h], jnp.concatenate([low, upper, lower], axis=0))


def sweep(k_ref, lhs, ridges, old, new, norms):
    after = []
    width, toks = old[0].shape[1:]
    for h in range(lhs.shape[0]):
        image = operator(k_ref, lhs, old[1], h)
        parts = []
        for c in range(0, toks, width):
            at = slice(c, c + width)
            direction = old[1][h, :, at]
            applied = image[:, at] + ridges[h] * direction
            norm = norms[h][:, at]
            alpha = norm / jnp.sum(direction * applied, axis=0, keepdims=True)
            residual = old[0][h, :, at] - alpha * applied
            new[0][h, :, at] = residual
            following = square_sum(residual, 0)
            step = alpha * direction
            new[2][h, :, at] = step if old[2] is None else old[2][h, :, at] + step
            new[1][h, :, at] = residual + (following / norm) * direction
            parts.append(following)
        after.append(jnp.concatenate(parts, axis=1))
    return tuple(after)


def cg_first_kernel(width, rounds, sweeps, k_ref, kt_ref, qt_ref, ridge_ref, *refs):
    totals = refs[:rounds]
    lhs, ridges, norm_ref, *state = refs[rounds:]
    heads, _, _ = qt_ref.shape
    part = width // 2
    inner = lax.broadcasted_iota(jnp.int32, (part, part), 0) < lax.broadcasted_iota(
        jnp.int32, (part, part), 1
    )
    ridge_t = (ridge_ref[...] + prefix(totals, lambda ref: load_diag(ref, heads * part))).T
    norms = []
    for h in range(heads):
        rows = slice(h * part, (h + 1) * part)
        upper = prefix(totals, lambda ref: ref[rows].astype(F32))
        turned = upper.T
        tri = upper[:, :part]
        tri_t = turned[:part]
        lhs[h, :part, :width] = jnp.concatenate(
            [jnp.where(inner, tri, tri_t), upper[:, part:]], axis=1
        ).astype(BF16)
        lhs[h, part:, :width] = jnp.concatenate(
            [turned[part:], jnp.where(inner, tri_t, tri)], axis=1
        ).astype(BF16)
        lhs[h, :, width:] = kt_ref[h]
        ridges[h] = jnp.broadcast_to(ridge_t[:, h : h + 1], (width, width))
        norms.append(square_sum(qt_ref[h], 0))
    fixed = (k_ref, lhs, ridges)
    norms = sweep(*fixed, (qt_ref, qt_ref, None), state, norms)
    norms = lax.fori_loop(1, sweeps, lambda _, now: sweep(*fixed, state, state, now), norms)
    norm_ref[...] = jnp.concatenate(norms, axis=0)


def cg_last_kernel(width, sweeps, k_ref, lhs, ridges, norm_ref, *refs):
    given, x_ref, state = refs[:3], refs[3], refs[4:]
    heads = lhs.shape[0]
    fixed = (k_ref, lhs, ridges)
    norms = tuple(norm_ref[h : h + 1] for h in range(heads))
    norms = sweep(*fixed, given, state, norms)
    norms = lax.fori_loop(1, sweeps, lambda _, now: sweep(*fixed, state, state, now), norms)
    for h in range(heads):
        direction = state[1][h]
        ridge = jnp.concatenate([ridges[h]] * (direction.shape[1] // width), axis=1)
        image = operator(k_ref, lhs, state[1], h) + ridge * direction
        alpha = norms[h] / jnp.sum(direction * image, axis=0, keepdims=True)
        x = state[2][h] + alpha * direction
        x_ref[:, h * width : (h + 1) * width] = x.astype(BF16).T


def read_kernel(width, spots, x_ref, k_ref, val_ref, near_ref, own_ref, far_ref, *refs):
    outs, tmp = refs[:spots], refs[spots]
    count = own_ref.shape[0]
    later = lax.axis_index("seq") & 1
    toks = k_ref.shape[0]
    rows = toks // spots
    me = lax.axis_index("head")
    keep = lax.broadcasted_iota(jnp.int32, (toks, toks), 0) >= lax.broadcasted_iota(
        jnp.int32, (toks, toks), 1
    )
    for h in range(k_ref.shape[1] // width):
        cols = slice(h * width, (h + 1) * width)
        x = x_ref[:, cols]
        state = jnp.where(later == h // count, own_ref[h % count], far_ref[h % count])
        near = near_ref[h].astype(F32) * later.astype(F32)
        state = (state.astype(F32) + near).astype(BF16)
        score = jnp.where(keep, dot(x, k_ref[:, cols], ((1,), (1,))), 0.0).astype(BF16)
        out = dot(x, state, ((1,), (1,))) + dot(score, val_ref[:, cols])
        tmp[:, cols] = out.astype(BF16)
    for k in range(spots):
        outs[k][...] = tmp[pl.ds(pl.multiple_of((me ^ k) * rows, rows), rows), :]


def norm_kernel(spots, *refs):
    pieces, gate_ref, out_ref = refs[:spots], refs[spots], refs[spots + 1]
    me = lax.axis_index("head")
    wide = pieces[0].shape[1]
    total = 0.0
    for k in range(spots):
        total = total + square_sum(pieces[k][...].astype(F32), 1)
    factor = lax.rsqrt(total / (wide * spots) + EPS)
    for k in range(spots):
        cols = pl.ds(pl.multiple_of((me ^ k) * wide, wide), wide)
        out_ref[:, cols] = (pieces[k][...].astype(F32) * factor * gate_ref[:, cols]).astype(BF16)


def swap(x, axis, size, step):
    return lax.ppermute(x, axis, [(i, i ^ step) for i in range(size)])


def shape(*dims, dtype=BF16):
    return jax.ShapeDtypeStruct(dims, dtype)


def shards(mesh, queries, key_rows, values, write_gate, ridge_diag, norm_gain, gate_logits):
    toks, cols = queries.shape
    heads = write_gate.shape[1]
    width = cols // heads
    spots = mesh.shape["head"]
    size = mesh.shape["seq"]
    rounds = size.bit_length() - 1
    rows = toks // spots
    gates = write_gate.T
    packed = heads * width // 2 + 2 * heads
    work = 2 * toks * width * width * heads

    kk, kt, keys, vals, scales = call(
        functools.partial(key_state_kernel, width),
        [
            shape(packed, width),
            shape(heads, width, toks),
            shape(toks, cols),
            shape(toks, cols),
            shape(heads, toks, dtype=F32),
        ],
        [pl.BlockSpec(memory_space=pltpu.MemorySpace.HBM)] * 3,
        [pltpu.VMEM((heads, toks), F32), pltpu.SemaphoreType.DMA((heads + 2,))],
        flops=work,
    )(
        *(
            pltpu.with_memory_space_constraint(x, pltpu.MemorySpace.HBM)
            for x in (key_rows, values, gates)
        )
    )
    vals, vk = call(
        functools.partial(value_state_kernel, width),
        [shape(toks, cols), shape(heads, width, width)],
        [VMEM] * 3,
        flops=work,
    )(keys, vals, scales)
    qt = call(
        functools.partial(prepare_kernel, width),
        shape(heads, width, toks, dtype=F32),
        [VMEM],
        mib=4,
        flops=work,
    )(queries)
    gated = call(gate_kernel, shape(*gate_logits.shape, dtype=F32), [VMEM] * 2, flops=work)(
        norm_gain[None, :], gate_logits
    )

    key_in, value_in = [], []
    for k in range(rounds):
        key_in.append(swap(kk, "seq", size, 1 << k))
        if k + 1 < rounds:
            kk = call(
                functools.partial(key_join_kernel, packed - 2 * heads),
                shape(packed, width),
                [VMEM] * 2,
                mib=4,
            )(kk, key_in[-1])
    near = swap(vk, "seq", size, 1)
    vk = call(value_fold_kernel, shape(heads // 2, width, width), [VMEM] * 2)(vk, near)
    for k in range(1, rounds):
        value_in.append(swap(vk, "seq", size, 1 << k))
        if k + 1 < rounds:
            vk = call(value_join_kernel, shape(*vk.shape), [VMEM] * 2)(vk, value_in[-1])
    own = call(value_prefix_kernel, shape(*vk.shape), [VMEM] * (rounds - 1))(*value_in)
    far = swap(own, "seq", size, 1)

    lhs, ridges, norms, *state = call(
        functools.partial(cg_first_kernel, width, rounds, FIRST),
        [
            shape(heads, width, width + toks),
            shape(heads, width, width, dtype=F32),
            shape(heads, toks, dtype=F32),
        ]
        + [shape(heads, width, toks, dtype=F32)] * 3,
        [VMEM] * (4 + rounds),
        mib=4,
        flops=10 * work,
    )(keys, kt, qt, ridge_diag, *key_in)
    x = call(
        functools.partial(cg_last_kernel, width, ITERS - 1 - FIRST),
        shape(toks, cols),
        [VMEM] * 7,
        [pltpu.VMEM((heads, width, toks), F32)] * 3,
        mib=8,
        flops=10 * work,
    )(keys, lhs, ridges, norms, *state)

    pieces = call(
        functools.partial(read_kernel, width, spots),
        [shape(rows, cols)] * spots,
        [VMEM] * 6,
        [pltpu.VMEM((toks, cols), BF16)],
        flops=work,
    )(x, keys, vals, near, own, far)
    arrived = [pieces[0]] + [swap(pieces[k], "head", spots, k) for k in range(1, spots)]
    return call(
        functools.partial(norm_kernel, spots),
        shape(rows, spots * cols),
        [VMEM] * (spots + 1),
        flops=work,
    )(*arrived, gated)


def solution(mesh):
    return jax.shard_map(
        functools.partial(shards, mesh),
        mesh=mesh,
        in_specs=(
            P("seq", "head"),
            P("seq", "head"),
            P("seq", "head"),
            P("seq", "head"),
            P("head", None),
            P(),
            P(("seq", "head"), None),
        ),
        out_specs=P(("seq", "head"), None),
        check_vma=False,
    )
```

```python
import functools

import jax
import jax.numpy as jnp
from jax import lax
from jax.experimental import pallas as pl
from jax.experimental.pallas import tpu as pltpu
from jax.sharding import PartitionSpec as P


ITERS = 8
FIRST = 4
EPS = 1e-06

F32 = jnp.float32
BF16 = jnp.bfloat16
VMEM = pl.BlockSpec(memory_space=pltpu.VMEM)


def call(body, shapes, specs, scratch=(), mib=4, flops=0):
    single = not isinstance(shapes, list)
    return pl.pallas_call(
        body,
        out_shape=shapes,
        in_specs=specs,
        out_specs=VMEM if single else [VMEM] * len(shapes),
        scratch_shapes=list(scratch),
        compiler_params=pltpu.CompilerParams(vmem_limit_bytes=mib << 20),
        cost_estimate=pl.CostEstimate(flops=flops, bytes_accessed=1 << 20, transcendentals=0),
    )


def dot(a, b, dims=((1,), (0,))):
    return lax.dot_general(a, b, (dims, ((), ())), preferred_element_type=F32)


def square_sum(block, axis):
    return jnp.sum(block * block, axis=axis, keepdims=True)


def key_state_kernel(width, k_hbm, v_hbm, gate_hbm, kk_ref, kt_ref, k_ref, v_ref, scale_ref, gate_ref, sems):
    heads = gate_ref.shape[0]
    half = width // 2
    loads = [pltpu.make_async_copy(gate_hbm, gate_ref, sems.at[heads])]
    for h in range(heads):
        cols = slice(h * width, (h + 1) * width)
        loads.append(pltpu.make_async_copy(k_hbm.at[:, cols], k_ref.at[:, cols], sems.at[h]))
    loads.append(pltpu.make_async_copy(v_hbm, v_ref, sems.at[heads + 1]))
    for load in loads:
        load.start()
    row = lax.broadcasted_iota(jnp.int32, (half, width), 0)
    col = lax.broadcasted_iota(jnp.int32, (half, width), 1)
    loads[0].wait()
    diags = []
    for h in range(heads):
        loads[1 + h].wait()
        key = k_ref[:, h * width : (h + 1) * width]
        turned = key.T.astype(F32)
        total = square_sum(turned, 0) + EPS
        scale_ref[h : h + 1] = gate_ref[h : h + 1] * lax.rsqrt(total)
        wide = (turned * (gate_ref[h : h + 1] / total)).astype(BF16)
        kt_ref[h] = wide
        kk = dot(wide, key)
        diag = jnp.where(row == col, kk[:half], jnp.where(row + half == col, kk[half:], 0.0))
        diags.append(jnp.sum(diag, axis=0, keepdims=True))
        other = pltpu.roll(kk[half:], half, 1)
        packed = jnp.where(row > col, other, jnp.where(row == col, 0.0, kk[:half]))
        kk_ref[h * half : (h + 1) * half] = packed.astype(BF16)
    store_diag(kk_ref, heads * half, jnp.concatenate(diags, axis=0))
    loads[-1].wait()


def store_diag(ref, at, diag):
    heads = diag.shape[0]
    high = diag.astype(BF16)
    ref[at : at + 2 * heads] = jnp.concatenate(
        [high, (diag - high.astype(F32)).astype(BF16)], axis=0
    )


def load_diag(ref, at):
    both = ref[at:].astype(F32)
    heads = both.shape[0] // 2
    return both[:heads] + both[heads:]


def key_join_kernel(at, mine_ref, other_ref, total_ref):
    total_ref[:at] = (mine_ref[:at].astype(F32) + other_ref[:at].astype(F32)).astype(BF16)
    store_diag(total_ref, at, load_diag(mine_ref, at) + load_diag(other_ref, at))


def value_join_kernel(mine_ref, other_ref, total_ref):
    total_ref[...] = (mine_ref[...].astype(F32) + other_ref[...].astype(F32)).astype(BF16)


def value_prefix_kernel(keep_ref, near_ref, *refs):
    later = (lax.axis_index("seq") & 1).astype(F32)
    before = prefix(refs[:-2], lambda ref: ref[...].astype(F32), 1)
    refs[-2][...] = (before + later * near_ref[...].astype(F32)).astype(BF16)
    refs[-1][...] = (before + (1.0 - later) * keep_ref[...].astype(F32)).astype(BF16)


def value_state_kernel(width, k_ref, v_ref, scale_ref, val_ref, keep_ref, give_ref):
    scales = scale_ref[...].T
    later = (lax.axis_index("seq") & 1) == 1
    count = keep_ref.shape[0]
    for h in range(count):
        pair = []
        for head in (h, count + h):
            cols = slice(head * width, (head + 1) * width)
            val = (v_ref[:, cols].astype(F32) * scales[:, head : head + 1]).astype(BF16)
            val_ref[:, cols] = val
            pair.append(dot(val, k_ref[:, cols], ((0,), (0,))))
        keep_ref[h] = jnp.where(later, pair[1], pair[0]).astype(BF16)
        give_ref[h] = jnp.where(later, pair[0], pair[1]).astype(BF16)


def prepare_kernel(width, q_ref, qt_ref):
    for h in range(qt_ref.shape[0]):
        query = q_ref[:, h * width : (h + 1) * width].T.astype(F32)
        qt_ref[h] = query * lax.rsqrt(square_sum(query, 0) + EPS)


def gate_kernel(gain_ref, logit_ref, out_ref):
    out_ref[...] = gain_ref[...] * jax.nn.sigmoid(logit_ref[...].astype(F32))


def prefix(refs, load, first=0):
    place = lax.axis_index("seq")
    total = 0.0
    for k, ref in enumerate(refs):
        total = total + load(ref) * ((place >> (first + k)) & 1).astype(F32)
    return total


def operator(k_ref, lhs, directions, h):
    _, width, toks = directions.shape
    half = toks // 2
    low = directions[h].astype(BF16)
    score = dot(k_ref[:, h * width : (h + 1) * width], low).astype(BF16)
    keep = lax.broadcasted_iota(jnp.int32, (half, half), 0) <= lax.broadcasted_iota(
        jnp.int32, (half, half), 1
    )
    none = jnp.zeros((half, half), BF16)
    upper = jnp.concatenate([jnp.where(keep, score[:half, :half], none), score[:half, half:]], axis=1)
    lower = jnp.concatenate([none, jnp.where(keep, score[half:, half:], none)], axis=1)
    return dot(lhs[h], jnp.concatenate([low, upper, lower], axis=0))


def sweep(k_ref, lhs, ridges, old, new, norms):
    after = []
    width, toks = old[0].shape[1:]
    for h in range(lhs.shape[0]):
        image = operator(k_ref, lhs, old[1], h)
        parts = []
        for c in range(0, toks, width):
            at = slice(c, c + width)
            direction = old[1][h, :, at]
            applied = image[:, at] + ridges[h] * direction
            norm = norms[h][:, at]
            alpha = norm / jnp.sum(direction * applied, axis=0, keepdims=True)
            residual = old[0][h, :, at] - alpha * applied
            new[0][h, :, at] = residual
            following = square_sum(residual, 0)
            step = alpha * direction
            new[2][h, :, at] = step if old[2] is None else old[2][h, :, at] + step
            new[1][h, :, at] = residual + (following / norm) * direction
            parts.append(following)
        after.append(jnp.concatenate(parts, axis=1))
    return tuple(after)


def cg_first_kernel(width, rounds, sweeps, k_ref, kt_ref, qt_ref, ridge_ref, *refs):
    totals = refs[:rounds]
    lhs, ridges, norm_ref, *state = refs[rounds:]
    heads, _, _ = qt_ref.shape
    part = width // 2
    inner = lax.broadcasted_iota(jnp.int32, (part, part), 0) < lax.broadcasted_iota(
        jnp.int32, (part, part), 1
    )
    ridge_t = (ridge_ref[...] + prefix(totals, lambda ref: load_diag(ref, heads * part))).T
    norms = []
    for h in range(heads):
        rows = slice(h * part, (h + 1) * part)
        upper = prefix(totals, lambda ref: ref[rows].astype(F32))
        turned = upper.T
        tri = upper[:, :part]
        tri_t = turned[:part]
        lhs[h, :part, :width] = jnp.concatenate(
            [jnp.where(inner, tri, tri_t), upper[:, part:]], axis=1
        ).astype(BF16)
        lhs[h, part:, :width] = jnp.concatenate(
            [turned[part:], jnp.where(inner, tri_t, tri)], axis=1
        ).astype(BF16)
        lhs[h, :, width:] = kt_ref[h]
        ridges[h] = jnp.broadcast_to(ridge_t[:, h : h + 1], (width, width))
        norms.append(square_sum(qt_ref[h], 0))
    fixed = (k_ref, lhs, ridges)
    norms = sweep(*fixed, (qt_ref, qt_ref, None), state, norms)
    norms = lax.fori_loop(1, sweeps, lambda _, now: sweep(*fixed, state, state, now), norms)
    norm_ref[...] = jnp.concatenate(norms, axis=0)


def cg_last_kernel(width, sweeps, k_ref, lhs, ridges, norm_ref, *refs):
    given, x_ref, state = refs[:3], refs[3], refs[4:]
    heads = lhs.shape[0]
    fixed = (k_ref, lhs, ridges)
    norms = tuple(norm_ref[h : h + 1] for h in range(heads))
    norms = sweep(*fixed, given, state, norms)
    norms = lax.fori_loop(1, sweeps, lambda _, now: sweep(*fixed, state, state, now), norms)
    for h in range(heads):
        direction = state[1][h]
        ridge = jnp.concatenate([ridges[h]] * (direction.shape[1] // width), axis=1)
        image = operator(k_ref, lhs, state[1], h) + ridge * direction
        alpha = norms[h] / jnp.sum(direction * image, axis=0, keepdims=True)
        x = state[2][h] + alpha * direction
        x_ref[:, h * width : (h + 1) * width] = x.astype(BF16).T


def read_kernel(width, spots, x_ref, k_ref, val_ref, own_ref, far_ref, *refs):
    outs, tmp = refs[:spots], refs[spots]
    count = own_ref.shape[0]
    later = lax.axis_index("seq") & 1
    toks = k_ref.shape[0]
    rows = toks // spots
    me = lax.axis_index("head")
    keep = lax.broadcasted_iota(jnp.int32, (toks, toks), 0) >= lax.broadcasted_iota(
        jnp.int32, (toks, toks), 1
    )
    for h in range(k_ref.shape[1] // width):
        cols = slice(h * width, (h + 1) * width)
        x = x_ref[:, cols]
        state = jnp.where(later == h // count, own_ref[h % count], far_ref[h % count])
        score = jnp.where(keep, dot(x, k_ref[:, cols], ((1,), (1,))), 0.0).astype(BF16)
        out = dot(x, state, ((1,), (1,))) + dot(score, val_ref[:, cols])
        tmp[:, cols] = out.astype(BF16)
    for k in range(spots):
        outs[k][...] = tmp[pl.ds(pl.multiple_of((me ^ k) * rows, rows), rows), :]


def norm_kernel(spots, *refs):
    pieces, gate_ref, out_ref = refs[:spots], refs[spots], refs[spots + 1]
    me = lax.axis_index("head")
    wide = pieces[0].shape[1]
    total = 0.0
    for k in range(spots):
        total = total + square_sum(pieces[k][...].astype(F32), 1)
    factor = lax.rsqrt(total / (wide * spots) + EPS)
    for k in range(spots):
        cols = pl.ds(pl.multiple_of((me ^ k) * wide, wide), wide)
        out_ref[:, cols] = (pieces[k][...].astype(F32) * factor * gate_ref[:, cols]).astype(BF16)


def swap(x, axis, size, step):
    return lax.ppermute(x, axis, [(i, i ^ step) for i in range(size)])


def shape(*dims, dtype=BF16):
    return jax.ShapeDtypeStruct(dims, dtype)


def shards(mesh, queries, key_rows, values, write_gate, ridge_diag, norm_gain, gate_logits):
    toks, cols = queries.shape
    heads = write_gate.shape[1]
    width = cols // heads
    spots = mesh.shape["head"]
    size = mesh.shape["seq"]
    rounds = size.bit_length() - 1
    rows = toks // spots
    gates = write_gate.T
    packed = heads * width // 2 + 2 * heads
    work = 2 * toks * width * width * heads

    kk, kt, keys, vals, scales = call(
        functools.partial(key_state_kernel, width),
        [
            shape(packed, width),
            shape(heads, width, toks),
            shape(toks, cols),
            shape(toks, cols),
            shape(heads, toks, dtype=F32),
        ],
        [pl.BlockSpec(memory_space=pltpu.MemorySpace.HBM)] * 3,
        [pltpu.VMEM((heads, toks), F32), pltpu.SemaphoreType.DMA((heads + 2,))],
        flops=work,
    )(
        *(
            pltpu.with_memory_space_constraint(x, pltpu.MemorySpace.HBM)
            for x in (key_rows, values, gates)
        )
    )
    vals, keep, give = call(
        functools.partial(value_state_kernel, width),
        [shape(toks, cols)] + [shape(heads // 2, width, width)] * 2,
        [VMEM] * 3,
        flops=work,
    )(keys, vals, scales)
    qt = call(
        functools.partial(prepare_kernel, width),
        shape(heads, width, toks, dtype=F32),
        [VMEM],
        mib=4,
        flops=work,
    )(queries)
    gated = call(gate_kernel, shape(*gate_logits.shape, dtype=F32), [VMEM] * 2, flops=work)(
        norm_gain[None, :], gate_logits
    )

    key_in, value_in = [], []
    for k in range(rounds):
        key_in.append(swap(kk, "seq", size, 1 << k))
        if k + 1 < rounds:
            kk = call(
                functools.partial(key_join_kernel, packed - 2 * heads),
                shape(packed, width),
                [VMEM] * 2,
                mib=4,
            )(kk, key_in[-1])
    near = swap(give, "seq", size, 1)
    vk = call(value_join_kernel, shape(*keep.shape), [VMEM] * 2)(keep, near)
    for k in range(1, rounds):
        value_in.append(swap(vk, "seq", size, 1 << k))
        if k + 1 < rounds:
            vk = call(value_join_kernel, shape(*vk.shape), [VMEM] * 2)(vk, value_in[-1])
    own, share = call(
        value_prefix_kernel, [shape(*vk.shape)] * 2, [VMEM] * (rounds + 1)
    )(keep, near, *value_in)
    far = swap(share, "seq", size, 1)

    lhs, ridges, norms, *state = call(
        functools.partial(cg_first_kernel, width, rounds, FIRST),
        [
            shape(heads, width, width + toks),
            shape(heads, width, width, dtype=F32),
            shape(heads, toks, dtype=F32),
        ]
        + [shape(heads, width, toks, dtype=F32)] * 3,
        [VMEM] * (4 + rounds),
        mib=4,
        flops=10 * work,
    )(keys, kt, qt, ridge_diag, *key_in)
    x = call(
        functools.partial(cg_last_kernel, width, ITERS - 1 - FIRST),
        shape(toks, cols),
        [VMEM] * 7,
        [pltpu.VMEM((heads, width, toks), F32)] * 3,
        mib=8,
        flops=10 * work,
    )(keys, lhs, ridges, norms, *state)

    pieces = call(
        functools.partial(read_kernel, width, spots),
        [shape(rows, cols)] * spots,
        [VMEM] * 5,
        [pltpu.VMEM((toks, cols), BF16)],
        flops=work,
    )(x, keys, vals, own, far)
    arrived = [pieces[0]] + [swap(pieces[k], "head", spots, k) for k in range(1, spots)]
    return call(
        functools.partial(norm_kernel, spots),
        shape(rows, spots * cols),
        [VMEM] * (spots + 1),
        flops=work,
    )(*arrived, gated)


def solution(mesh):
    return jax.shard_map(
        functools.partial(shards, mesh),
        mesh=mesh,
        in_specs=(
            P("seq", "head"),
            P("seq", "head"),
            P("seq", "head"),
            P("seq", "head"),
            P("head", None),
            P(),
            P(("seq", "head"), None),
        ),
        out_specs=P(("seq", "head"), None),
        check_vma=False,
    )
```

```python
import functools

import jax
import jax.numpy as jnp
from jax import lax
from jax.experimental import pallas as pl
from jax.experimental.pallas import tpu as pltpu
from jax.sharding import PartitionSpec as P


ITERS = 8
FIRST = 5
EPS = 1e-06

F32 = jnp.float32
BF16 = jnp.bfloat16
VMEM = pl.BlockSpec(memory_space=pltpu.VMEM)


def call(body, shapes, specs, scratch=(), mib=4, flops=0):
    single = not isinstance(shapes, list)
    return pl.pallas_call(
        body,
        out_shape=shapes,
        in_specs=specs,
        out_specs=VMEM if single else [VMEM] * len(shapes),
        scratch_shapes=list(scratch),
        compiler_params=pltpu.CompilerParams(vmem_limit_bytes=mib << 20),
        cost_estimate=pl.CostEstimate(flops=flops, bytes_accessed=1 << 20, transcendentals=0),
    )


def dot(a, b, dims=((1,), (0,))):
    return lax.dot_general(a, b, (dims, ((), ())), preferred_element_type=F32)


def square_sum(block, axis):
    return jnp.sum(block * block, axis=axis, keepdims=True)


def key_state_kernel(width, k_hbm, v_hbm, gate_hbm, kk_ref, kt_ref, k_ref, v_ref, scale_ref, gate_ref, sems):
    heads = gate_ref.shape[0]
    half = width // 2
    loads = [pltpu.make_async_copy(gate_hbm, gate_ref, sems.at[0])]
    loads.append(pltpu.make_async_copy(k_hbm, k_ref, sems.at[1]))
    loads.append(pltpu.make_async_copy(v_hbm, v_ref, sems.at[2]))
    for load in loads:
        load.start()
    row = lax.broadcasted_iota(jnp.int32, (half, width), 0)
    col = lax.broadcasted_iota(jnp.int32, (half, width), 1)
    loads[0].wait()
    loads[1].wait()
    diags = []
    for h in range(heads):
        key = k_ref[:, h * width : (h + 1) * width]
        turned = key.T.astype(F32)
        total = square_sum(turned, 0) + EPS
        scale_ref[h : h + 1] = gate_ref[h : h + 1] * lax.rsqrt(total)
        wide = (turned * (gate_ref[h : h + 1] / total)).astype(BF16)
        kt_ref[h] = wide
        kk = dot(wide, key)
        diag = jnp.where(row == col, kk[:half], jnp.where(row + half == col, kk[half:], 0.0))
        diags.append(jnp.sum(diag, axis=0, keepdims=True))
        other = pltpu.roll(kk[half:], half, 1)
        packed = jnp.where(row > col, other, jnp.where(row == col, 0.0, kk[:half]))
        kk_ref[h * half : (h + 1) * half] = packed.astype(BF16)
    store_diag(kk_ref, heads * half, jnp.concatenate(diags, axis=0))
    loads[2].wait()


def store_diag(ref, at, diag):
    heads = diag.shape[0]
    high = diag.astype(BF16)
    ref[at : at + 2 * heads] = jnp.concatenate(
        [high, (diag - high.astype(F32)).astype(BF16)], axis=0
    )


def load_diag(ref, at):
    both = ref[at:].astype(F32)
    heads = both.shape[0] // 2
    return both[:heads] + both[heads:]


def key_join_kernel(at, mine_ref, other_ref, total_ref):
    total_ref[:at] = (mine_ref[:at].astype(F32) + other_ref[:at].astype(F32)).astype(BF16)
    store_diag(total_ref, at, load_diag(mine_ref, at) + load_diag(other_ref, at))


def value_join_kernel(mine_ref, other_ref, total_ref):
    total_ref[...] = (mine_ref[...].astype(F32) + other_ref[...].astype(F32)).astype(BF16)


def value_prefix_kernel(keep_ref, near_ref, *refs):
    later = (lax.axis_index("seq") & 1).astype(F32)
    before = prefix(refs[:-2], lambda ref: ref[...].astype(F32), 1)
    refs[-2][...] = (before + later * near_ref[...].astype(F32)).astype(BF16)
    refs[-1][...] = (before + (1.0 - later) * keep_ref[...].astype(F32)).astype(BF16)


def value_state_kernel(width, k_ref, v_ref, scale_ref, val_ref, keep_ref, give_ref):
    scales = scale_ref[...].T
    later = (lax.axis_index("seq") & 1) == 1
    count = keep_ref.shape[0]
    for h in range(count):
        pair = []
        for head in (h, count + h):
            cols = slice(head * width, (head + 1) * width)
            val = (v_ref[:, cols].astype(F32) * scales[:, head : head + 1]).astype(BF16)
            val_ref[:, cols] = val
            pair.append(dot(val, k_ref[:, cols], ((0,), (0,))))
        keep_ref[h] = jnp.where(later, pair[1], pair[0]).astype(BF16)
        give_ref[h] = jnp.where(later, pair[0], pair[1]).astype(BF16)


def causal(k_ref, low, h):
    width, toks = low.shape
    half = toks // 2
    score = dot(k_ref[:, h * width : (h + 1) * width], low).astype(BF16)
    keep = lax.broadcasted_iota(jnp.int32, (half, half), 0) <= lax.broadcasted_iota(
        jnp.int32, (half, half), 1
    )
    none = jnp.zeros((half, half), BF16)
    upper = jnp.concatenate([jnp.where(keep, score[:half, :half], none), score[:half, half:]], axis=1)
    lower = jnp.concatenate([none, jnp.where(keep, score[half:, half:], none)], axis=1)
    return [upper, lower]


def prepare_kernel(width, q_ref, k_ref, kt_ref, qt_ref, local_ref):
    for h in range(qt_ref.shape[0]):
        query = q_ref[:, h * width : (h + 1) * width].T.astype(F32)
        query = query * lax.rsqrt(square_sum(query, 0) + EPS)
        qt_ref[h] = query
        scores = jnp.concatenate(causal(k_ref, query.astype(BF16), h), axis=0)
        local_ref[h] = dot(kt_ref[h], scores)


def gate_kernel(gain_ref, logit_ref, out_ref):
    out_ref[...] = gain_ref[...] * jax.nn.sigmoid(logit_ref[...].astype(F32))


def prefix(refs, load, first=0):
    place = lax.axis_index("seq")
    total = 0.0
    for k, ref in enumerate(refs):
        total = total + load(ref) * ((place >> (first + k)) & 1).astype(F32)
    return total


def operator(k_ref, kt_ref, mat_ref, directions, h):
    low = directions[h].astype(BF16)
    both = jnp.concatenate([mat_ref[h], kt_ref[h]], axis=1)
    return dot(both, jnp.concatenate([low] + causal(k_ref, low, h), axis=0))


def sweep(k_ref, kt_ref, mat_ref, ridges, old, new, norms, local=None):
    after = []
    width, toks = old[0].shape[1:]
    for h in range(mat_ref.shape[0]):
        if local is None:
            image = operator(k_ref, kt_ref, mat_ref, old[1], h)
        else:
            image = local[h] + dot(mat_ref[h], old[1][h].astype(BF16))
        parts = []
        for c in range(0, toks, width):
            at = slice(c, c + width)
            direction = old[1][h, :, at]
            applied = image[:, at] + ridges[h] * direction
            norm = norms[h][:, at]
            alpha = norm / jnp.sum(direction * applied, axis=0, keepdims=True)
            residual = old[0][h, :, at] - alpha * applied
            new[0][h, :, at] = residual
            following = square_sum(residual, 0)
            step = alpha * direction
            new[2][h, :, at] = step if old[2] is None else old[2][h, :, at] + step
            new[1][h, :, at] = residual + (following / norm) * direction
            parts.append(following)
        after.append(jnp.concatenate(parts, axis=1))
    return tuple(after)


def cg_first_kernel(width, rounds, sweeps, k_ref, kt_ref, qt_ref, local_ref, ridge_ref, *refs):
    totals = refs[:rounds]
    mat_ref, ridges, norm_ref, *state = refs[rounds:]
    heads, _, _ = qt_ref.shape
    part = width // 2
    inner = lax.broadcasted_iota(jnp.int32, (part, part), 0) < lax.broadcasted_iota(
        jnp.int32, (part, part), 1
    )
    ridge_t = (ridge_ref[...] + prefix(totals, lambda ref: load_diag(ref, heads * part))).T
    norms = []
    for h in range(heads):
        rows = slice(h * part, (h + 1) * part)
        upper = prefix(totals, lambda ref: ref[rows].astype(F32))
        turned = upper.T
        tri = upper[:, :part]
        tri_t = turned[:part]
        mat_ref[h, :part] = jnp.concatenate(
            [jnp.where(inner, tri, tri_t), upper[:, part:]], axis=1
        ).astype(BF16)
        mat_ref[h, part:] = jnp.concatenate(
            [turned[part:], jnp.where(inner, tri_t, tri)], axis=1
        ).astype(BF16)
        ridges[h] = jnp.broadcast_to(ridge_t[:, h : h + 1], (width, width))
        norms.append(square_sum(qt_ref[h], 0))
    fixed = (k_ref, kt_ref, mat_ref, ridges)
    norms = sweep(*fixed, (qt_ref, qt_ref, None), state, norms, local_ref)
    norms = lax.fori_loop(1, sweeps, lambda _, now: sweep(*fixed, state, state, now), norms)
    norm_ref[...] = jnp.concatenate(norms, axis=0)


def cg_last_kernel(width, sweeps, k_ref, kt_ref, mat_ref, ridges, norm_ref, *refs):
    given, x_ref, state = refs[:3], refs[3], refs[4:]
    heads = mat_ref.shape[0]
    fixed = (k_ref, kt_ref, mat_ref, ridges)
    norms = tuple(norm_ref[h : h + 1] for h in range(heads))
    norms = sweep(*fixed, given, state, norms)
    norms = lax.fori_loop(1, sweeps, lambda _, now: sweep(*fixed, state, state, now), norms)
    for h in range(heads):
        direction = state[1][h]
        ridge = jnp.concatenate([ridges[h]] * (direction.shape[1] // width), axis=1)
        image = operator(k_ref, kt_ref, mat_ref, state[1], h) + ridge * direction
        alpha = norms[h] / jnp.sum(direction * image, axis=0, keepdims=True)
        x = state[2][h] + alpha * direction
        x_ref[:, h * width : (h + 1) * width] = x.astype(BF16).T


def read_kernel(width, spots, x_ref, k_ref, val_ref, own_ref, far_ref, *refs):
    outs, tmp = refs[:spots], refs[spots]
    count = own_ref.shape[0]
    later = lax.axis_index("seq") & 1
    toks = k_ref.shape[0]
    rows = toks // spots
    me = lax.axis_index("head")
    keep = lax.broadcasted_iota(jnp.int32, (toks, toks), 0) >= lax.broadcasted_iota(
        jnp.int32, (toks, toks), 1
    )
    for h in range(k_ref.shape[1] // width):
        cols = slice(h * width, (h + 1) * width)
        x = x_ref[:, cols]
        state = jnp.where(later == h // count, own_ref[h % count], far_ref[h % count])
        score = jnp.where(keep, dot(x, k_ref[:, cols], ((1,), (1,))), 0.0).astype(BF16)
        out = dot(x, state, ((1,), (1,))) + dot(score, val_ref[:, cols])
        tmp[:, cols] = out.astype(BF16)
    for k in range(spots):
        outs[k][...] = tmp[pl.ds(pl.multiple_of((me ^ k) * rows, rows), rows), :]


def norm_kernel(spots, *refs):
    pieces, gate_ref, out_ref = refs[:spots], refs[spots], refs[spots + 1]
    me = lax.axis_index("head")
    wide = pieces[0].shape[1]
    total = 0.0
    for k in range(spots):
        total = total + square_sum(pieces[k][...].astype(F32), 1)
    factor = lax.rsqrt(total / (wide * spots) + EPS)
    for k in range(spots):
        cols = pl.ds(pl.multiple_of((me ^ k) * wide, wide), wide)
        out_ref[:, cols] = (pieces[k][...].astype(F32) * factor * gate_ref[:, cols]).astype(BF16)


def swap(x, axis, size, step):
    return lax.ppermute(x, axis, [(i, i ^ step) for i in range(size)])


def shape(*dims, dtype=BF16):
    return jax.ShapeDtypeStruct(dims, dtype)


def shards(mesh, queries, key_rows, values, write_gate, ridge_diag, norm_gain, gate_logits):
    toks, cols = queries.shape
    heads = write_gate.shape[1]
    width = cols // heads
    spots = mesh.shape["head"]
    size = mesh.shape["seq"]
    rounds = size.bit_length() - 1
    rows = toks // spots
    gates = write_gate.T
    packed = heads * width // 2 + 2 * heads
    work = 2 * toks * width * width * heads

    kk, kt, keys, vals, scales = call(
        functools.partial(key_state_kernel, width),
        [
            shape(packed, width),
            shape(heads, width, toks),
            shape(toks, cols),
            shape(toks, cols),
            shape(heads, toks, dtype=F32),
        ],
        [pl.BlockSpec(memory_space=pltpu.MemorySpace.HBM)] * 3,
        [pltpu.VMEM((heads, toks), F32), pltpu.SemaphoreType.DMA((3,))],
        flops=work,
    )(
        *(
            pltpu.with_memory_space_constraint(x, pltpu.MemorySpace.HBM)
            for x in (key_rows, values, gates)
        )
    )
    vals, keep, give = call(
        functools.partial(value_state_kernel, width),
        [shape(toks, cols)] + [shape(heads // 2, width, width)] * 2,
        [VMEM] * 3,
        flops=work,
    )(keys, vals, scales)
    qt, local = call(
        functools.partial(prepare_kernel, width),
        [shape(heads, width, toks, dtype=F32)] * 2,
        [VMEM] * 3,
        mib=4,
        flops=work,
    )(queries, keys, kt)
    gated = call(gate_kernel, shape(*gate_logits.shape, dtype=F32), [VMEM] * 2, flops=work)(
        norm_gain[None, :], gate_logits
    )

    key_in, value_in = [], []
    for k in range(rounds):
        key_in.append(swap(kk, "seq", size, 1 << k))
        if k + 1 < rounds:
            kk = call(
                functools.partial(key_join_kernel, packed - 2 * heads),
                shape(packed, width),
                [VMEM] * 2,
                mib=4,
            )(kk, key_in[-1])
    near = swap(give, "seq", size, 1)
    vk = call(value_join_kernel, shape(*keep.shape), [VMEM] * 2)(keep, near)
    for k in range(1, rounds):
        value_in.append(swap(vk, "seq", size, 1 << k))
        if k + 1 < rounds:
            vk = call(value_join_kernel, shape(*vk.shape), [VMEM] * 2)(vk, value_in[-1])
    own, share = call(
        value_prefix_kernel, [shape(*vk.shape)] * 2, [VMEM] * (rounds + 1)
    )(keep, near, *value_in)
    far = swap(share, "seq", size, 1)

    mat, ridges, norms, *state = call(
        functools.partial(cg_first_kernel, width, rounds, FIRST),
        [
            shape(heads, width, width),
            shape(heads, width, width, dtype=F32),
            shape(heads, toks, dtype=F32),
        ]
        + [shape(heads, width, toks, dtype=F32)] * 3,
        [VMEM] * (5 + rounds),
        mib=4,
        flops=10 * work,
    )(keys, kt, qt, local, ridge_diag, *key_in)
    x = call(
        functools.partial(cg_last_kernel, width, ITERS - 1 - FIRST),
        shape(toks, cols),
        [VMEM] * 8,
        [pltpu.VMEM((heads, width, toks), F32)] * 3,
        mib=8,
        flops=10 * work,
    )(keys, kt, mat, ridges, norms, *state)

    pieces = call(
        functools.partial(read_kernel, width, spots),
        [shape(rows, cols)] * spots,
        [VMEM] * 5,
        [pltpu.VMEM((toks, cols), BF16)],
        flops=work,
    )(x, keys, vals, own, far)
    arrived = [pieces[0]] + [swap(pieces[k], "head", spots, k) for k in range(1, spots)]
    return call(
        functools.partial(norm_kernel, spots),
        shape(rows, spots * cols),
        [VMEM] * (spots + 1),
        flops=work,
    )(*arrived, gated)


def solution(mesh):
    return jax.shard_map(
        functools.partial(shards, mesh),
        mesh=mesh,
        in_specs=(
            P("seq", "head"),
            P("seq", "head"),
            P("seq", "head"),
            P("seq", "head"),
            P("head", None),
            P(),
            P(("seq", "head"), None),
        ),
        out_specs=P(("seq", "head"), None),
        check_vma=False,
    )
```

```python
import functools

import jax
import jax.numpy as jnp
from jax import lax
from jax.experimental import pallas as pl
from jax.experimental.pallas import tpu as pltpu
from jax.sharding import PartitionSpec as P


ITERS = 8
FIRST = 5
EPS = 1e-06

F32 = jnp.float32
BF16 = jnp.bfloat16
VMEM = pl.BlockSpec(memory_space=pltpu.VMEM)


def call(body, shapes, specs, scratch=(), mib=4, flops=0):
    single = not isinstance(shapes, list)
    return pl.pallas_call(
        body,
        out_shape=shapes,
        in_specs=specs,
        out_specs=VMEM if single else [VMEM] * len(shapes),
        scratch_shapes=list(scratch),
        compiler_params=pltpu.CompilerParams(vmem_limit_bytes=mib << 20),
        cost_estimate=pl.CostEstimate(flops=flops, bytes_accessed=1 << 20, transcendentals=0),
    )


def dot(a, b, dims=((1,), (0,))):
    return lax.dot_general(a, b, (dims, ((), ())), preferred_element_type=F32)


def square_sum(block, axis):
    return jnp.sum(block * block, axis=axis, keepdims=True)


def key_state_kernel(width, k_hbm, v_hbm, gate_hbm, keep_ref, give_ref, kt_ref, k_ref, v_ref, scale_ref, gate_ref, sems):
    heads = gate_ref.shape[0]
    half = width // 2
    loads = [pltpu.make_async_copy(gate_hbm, gate_ref, sems.at[0])]
    loads.append(pltpu.make_async_copy(k_hbm, k_ref, sems.at[1]))
    loads.append(pltpu.make_async_copy(v_hbm, v_ref, sems.at[2]))
    for load in loads:
        load.start()
    row = lax.broadcasted_iota(jnp.int32, (half, width), 0)
    col = lax.broadcasted_iota(jnp.int32, (half, width), 1)
    loads[0].wait()
    loads[1].wait()
    later = (lax.axis_index("seq") & 1) == 1
    count = heads // 2
    blocks, diags = [], []
    for h in range(heads):
        key = k_ref[:, h * width : (h + 1) * width]
        turned = key.T.astype(F32)
        total = square_sum(turned, 0) + EPS
        scale_ref[h : h + 1] = gate_ref[h : h + 1] * lax.rsqrt(total)
        wide = (turned * (gate_ref[h : h + 1] / total)).astype(BF16)
        kt_ref[h] = wide
        kk = dot(wide, key)
        diag = jnp.where(row == col, kk[:half], jnp.where(row + half == col, kk[half:], 0.0))
        diags.append(jnp.sum(diag, axis=0, keepdims=True))
        other = pltpu.roll(kk[half:], half, 1)
        packed = jnp.where(row > col, other, jnp.where(row == col, 0.0, kk[:half]))
        blocks.append(packed.astype(BF16))
    for h in range(count):
        rows = slice(h * half, (h + 1) * half)
        keep_ref[rows] = jnp.where(later, blocks[count + h], blocks[h])
        give_ref[rows] = jnp.where(later, blocks[h], blocks[count + h])
    low, high = jnp.concatenate(diags[:count], axis=0), jnp.concatenate(diags[count:], axis=0)
    store_diag(keep_ref, count * half, jnp.where(later, high, low))
    store_diag(give_ref, count * half, jnp.where(later, low, high))
    loads[2].wait()


def store_diag(ref, at, diag):
    heads = diag.shape[0]
    high = diag.astype(BF16)
    ref[at : at + 2 * heads] = jnp.concatenate(
        [high, (diag - high.astype(F32)).astype(BF16)], axis=0
    )


def load_diag(ref, at):
    both = ref[at:].astype(F32)
    heads = both.shape[0] // 2
    return both[:heads] + both[heads:]


def key_join_kernel(at, mine_ref, other_ref, total_ref):
    total_ref[:at] = (mine_ref[:at].astype(F32) + other_ref[:at].astype(F32)).astype(BF16)
    store_diag(total_ref, at, load_diag(mine_ref, at) + load_diag(other_ref, at))


def key_prefix_kernel(at, keep_ref, near_ref, *refs):
    later = (lax.axis_index("seq") & 1).astype(F32)
    for load, store in (
        (lambda ref: ref[:at].astype(F32), lambda ref, x: ref.__setitem__(slice(0, at), x.astype(BF16))),
        (lambda ref: load_diag(ref, at), lambda ref, x: store_diag(ref, at, x)),
    ):
        before = prefix(refs[:-2], load, 1)
        store(refs[-2], before + later * load(near_ref))
        store(refs[-1], before + (1.0 - later) * load(keep_ref))


def value_join_kernel(mine_ref, other_ref, total_ref):
    total_ref[...] = (mine_ref[...].astype(F32) + other_ref[...].astype(F32)).astype(BF16)


def value_prefix_kernel(keep_ref, near_ref, *refs):
    later = (lax.axis_index("seq") & 1).astype(F32)
    before = prefix(refs[:-2], lambda ref: ref[...].astype(F32), 1)
    refs[-2][...] = (before + later * near_ref[...].astype(F32)).astype(BF16)
    refs[-1][...] = (before + (1.0 - later) * keep_ref[...].astype(F32)).astype(BF16)


def value_state_kernel(width, k_ref, v_ref, scale_ref, val_ref, keep_ref, give_ref):
    scales = scale_ref[...].T
    later = (lax.axis_index("seq") & 1) == 1
    count = keep_ref.shape[0]
    for h in range(count):
        pair = []
        for head in (h, count + h):
            cols = slice(head * width, (head + 1) * width)
            val = (v_ref[:, cols].astype(F32) * scales[:, head : head + 1]).astype(BF16)
            val_ref[:, cols] = val
            pair.append(dot(val, k_ref[:, cols], ((0,), (0,))))
        keep_ref[h] = jnp.where(later, pair[1], pair[0]).astype(BF16)
        give_ref[h] = jnp.where(later, pair[0], pair[1]).astype(BF16)


def causal(k_ref, low, h):
    width, toks = low.shape
    half = toks // 2
    score = dot(k_ref[:, h * width : (h + 1) * width], low).astype(BF16)
    keep = lax.broadcasted_iota(jnp.int32, (half, half), 0) <= lax.broadcasted_iota(
        jnp.int32, (half, half), 1
    )
    none = jnp.zeros((half, half), BF16)
    upper = jnp.concatenate([jnp.where(keep, score[:half, :half], none), score[:half, half:]], axis=1)
    lower = jnp.concatenate([none, jnp.where(keep, score[half:, half:], none)], axis=1)
    return [upper, lower]


def prepare_kernel(width, q_ref, k_ref, kt_ref, qt_ref, local_ref):
    for h in range(qt_ref.shape[0]):
        query = q_ref[:, h * width : (h + 1) * width].T.astype(F32)
        query = query * lax.rsqrt(square_sum(query, 0) + EPS)
        qt_ref[h] = query
        scores = jnp.concatenate(causal(k_ref, query.astype(BF16), h), axis=0)
        local_ref[h] = dot(kt_ref[h], scores)


def gate_kernel(gain_ref, logit_ref, out_ref):
    out_ref[...] = gain_ref[...] * jax.nn.sigmoid(logit_ref[...].astype(F32))


def prefix(refs, load, first=0):
    place = lax.axis_index("seq")
    total = 0.0
    for k, ref in enumerate(refs):
        total = total + load(ref) * ((place >> (first + k)) & 1).astype(F32)
    return total


def operator(k_ref, kt_ref, mat_ref, directions, h):
    low = directions[h].astype(BF16)
    both = jnp.concatenate([mat_ref[h], kt_ref[h]], axis=1)
    return dot(both, jnp.concatenate([low] + causal(k_ref, low, h), axis=0))


def sweep(k_ref, kt_ref, mat_ref, ridges, old, new, norms, local=None):
    after = []
    width, toks = old[0].shape[1:]
    for h in range(mat_ref.shape[0]):
        if local is None:
            image = operator(k_ref, kt_ref, mat_ref, old[1], h)
        else:
            image = local[h] + dot(mat_ref[h], old[1][h].astype(BF16))
        parts = []
        for c in range(0, toks, width):
            at = slice(c, c + width)
            direction = old[1][h, :, at]
            applied = image[:, at] + ridges[h] * direction
            norm = norms[h][:, at]
            alpha = norm / jnp.sum(direction * applied, axis=0, keepdims=True)
            residual = old[0][h, :, at] - alpha * applied
            new[0][h, :, at] = residual
            following = square_sum(residual, 0)
            step = alpha * direction
            new[2][h, :, at] = step if old[2] is None else old[2][h, :, at] + step
            new[1][h, :, at] = residual + (following / norm) * direction
            parts.append(following)
        after.append(jnp.concatenate(parts, axis=1))
    return tuple(after)


def cg_first_kernel(width, sweeps, k_ref, kt_ref, qt_ref, local_ref, ridge_ref, own_ref, far_ref, *refs):
    mat_ref, ridges, norm_ref, *state = refs
    heads, _, _ = qt_ref.shape
    part = width // 2
    inner = lax.broadcasted_iota(jnp.int32, (part, part), 0) < lax.broadcasted_iota(
        jnp.int32, (part, part), 1
    )
    count = heads // 2
    own_diag, far_diag = load_diag(own_ref, count * part), load_diag(far_ref, count * part)
    later = (lax.axis_index("seq") & 1) == 1
    low = jnp.where(later, far_diag, own_diag)
    high = jnp.where(later, own_diag, far_diag)
    ridge_t = (ridge_ref[...] + jnp.concatenate([low, high], axis=0)).T
    norms = []
    for h in range(heads):
        rows = slice(h % count * part, (h % count + 1) * part)
        first, second = (own_ref, far_ref) if h < count else (far_ref, own_ref)
        upper = jnp.where(later, second[rows], first[rows]).astype(F32)
        turned = upper.T
        tri = upper[:, :part]
        tri_t = turned[:part]
        mat_ref[h, :part] = jnp.concatenate(
            [jnp.where(inner, tri, tri_t), upper[:, part:]], axis=1
        ).astype(BF16)
        mat_ref[h, part:] = jnp.concatenate(
            [turned[part:], jnp.where(inner, tri_t, tri)], axis=1
        ).astype(BF16)
        ridges[h] = jnp.broadcast_to(ridge_t[:, h : h + 1], (width, width))
        norms.append(square_sum(qt_ref[h], 0))
    fixed = (k_ref, kt_ref, mat_ref, ridges)
    norms = sweep(*fixed, (qt_ref, qt_ref, None), state, norms, local_ref)
    norms = lax.fori_loop(1, sweeps, lambda _, now: sweep(*fixed, state, state, now), norms)
    norm_ref[...] = jnp.concatenate(norms, axis=0)


def cg_last_kernel(width, sweeps, k_ref, kt_ref, mat_ref, ridges, norm_ref, *refs):
    given, x_ref, state = refs[:3], refs[3], refs[4:]
    heads = mat_ref.shape[0]
    fixed = (k_ref, kt_ref, mat_ref, ridges)
    norms = tuple(norm_ref[h : h + 1] for h in range(heads))
    norms = sweep(*fixed, given, state, norms)
    norms = lax.fori_loop(1, sweeps, lambda _, now: sweep(*fixed, state, state, now), norms)
    for h in range(heads):
        direction = state[1][h]
        ridge = jnp.concatenate([ridges[h]] * (direction.shape[1] // width), axis=1)
        image = operator(k_ref, kt_ref, mat_ref, state[1], h) + ridge * direction
        alpha = norms[h] / jnp.sum(direction * image, axis=0, keepdims=True)
        x = state[2][h] + alpha * direction
        x_ref[:, h * width : (h + 1) * width] = x.astype(BF16).T


def local_read_kernel(width, x_ref, k_ref, val_ref, local_ref):
    toks = k_ref.shape[0]
    keep = lax.broadcasted_iota(jnp.int32, (toks, toks), 0) >= lax.broadcasted_iota(
        jnp.int32, (toks, toks), 1
    )
    for h in range(k_ref.shape[1] // width):
        cols = slice(h * width, (h + 1) * width)
        score = jnp.where(keep, dot(x_ref[:, cols], k_ref[:, cols], ((1,), (1,))), 0.0)
        local_ref[:, cols] = dot(score.astype(BF16), val_ref[:, cols])


def read_kernel(width, spots, x_ref, local_ref, own_ref, far_ref, *refs):
    outs, tmp = refs[:spots], refs[spots]
    count = own_ref.shape[0]
    later = lax.axis_index("seq") & 1
    rows = x_ref.shape[0] // spots
    me = lax.axis_index("head")
    for h in range(x_ref.shape[1] // width):
        cols = slice(h * width, (h + 1) * width)
        state = jnp.where(later == h // count, own_ref[h % count], far_ref[h % count])
        out = dot(x_ref[:, cols], state, ((1,), (1,))) + local_ref[:, cols]
        tmp[:, cols] = out.astype(BF16)
    for k in range(spots):
        outs[k][...] = tmp[pl.ds(pl.multiple_of((me ^ k) * rows, rows), rows), :]


def norm_kernel(spots, *refs):
    pieces, gate_ref, out_ref = refs[:spots], refs[spots], refs[spots + 1]
    me = lax.axis_index("head")
    wide = pieces[0].shape[1]
    total = 0.0
    for k in range(spots):
        total = total + square_sum(pieces[k][...].astype(F32), 1)
    factor = lax.rsqrt(total / (wide * spots) + EPS)
    for k in range(spots):
        cols = pl.ds(pl.multiple_of((me ^ k) * wide, wide), wide)
        out_ref[:, cols] = (pieces[k][...].astype(F32) * factor * gate_ref[:, cols]).astype(BF16)


def swap(x, axis, size, step):
    return lax.ppermute(x, axis, [(i, i ^ step) for i in range(size)])


def shape(*dims, dtype=BF16):
    return jax.ShapeDtypeStruct(dims, dtype)


def shards(mesh, queries, key_rows, values, write_gate, ridge_diag, norm_gain, gate_logits):
    toks, cols = queries.shape
    heads = write_gate.shape[1]
    width = cols // heads
    spots = mesh.shape["head"]
    size = mesh.shape["seq"]
    rounds = size.bit_length() - 1
    rows = toks // spots
    gates = write_gate.T
    tall = heads // 2 * width // 2
    packed = tall + heads
    work = 2 * toks * width * width * heads

    keep, give, kt, keys, vals, scales = call(
        functools.partial(key_state_kernel, width),
        [
            shape(packed, width),
            shape(packed, width),
            shape(heads, width, toks),
            shape(toks, cols),
            shape(toks, cols),
            shape(heads, toks, dtype=F32),
        ],
        [pl.BlockSpec(memory_space=pltpu.MemorySpace.HBM)] * 3,
        [pltpu.VMEM((heads, toks), F32), pltpu.SemaphoreType.DMA((3,))],
        flops=work,
    )(
        *(
            pltpu.with_memory_space_constraint(x, pltpu.MemorySpace.HBM)
            for x in (key_rows, values, gates)
        )
    )
    vals, value_keep, value_give = call(
        functools.partial(value_state_kernel, width),
        [shape(toks, cols)] + [shape(heads // 2, width, width)] * 2,
        [VMEM] * 3,
        flops=work,
    )(keys, vals, scales)
    qt, local = call(
        functools.partial(prepare_kernel, width),
        [shape(heads, width, toks, dtype=F32)] * 2,
        [VMEM] * 3,
        mib=4,
        flops=work,
    )(queries, keys, kt)
    gated = call(gate_kernel, shape(*gate_logits.shape, dtype=F32), [VMEM] * 2, flops=work)(
        norm_gain[None, :], gate_logits
    )

    key_in, value_in = [], []
    near = swap(give, "seq", size, 1)
    kk = keep
    for k in range(1, rounds):
        kk = call(
            functools.partial(key_join_kernel, tall), shape(packed, width), [VMEM] * 2
        )(kk, key_in[-1] if key_in else near)
        key_in.append(swap(kk, "seq", size, 1 << k))
    key_own, share = call(
        functools.partial(key_prefix_kernel, tall),
        [shape(packed, width)] * 2,
        [VMEM] * (rounds + 1),
    )(keep, near, *key_in)
    key_far = swap(share, "seq", size, 1)

    keep = value_keep
    near = swap(value_give, "seq", size, 1)
    vk = call(value_join_kernel, shape(*keep.shape), [VMEM] * 2)(keep, near)
    for k in range(1, rounds):
        value_in.append(swap(vk, "seq", size, 1 << k))
        if k + 1 < rounds:
            vk = call(value_join_kernel, shape(*vk.shape), [VMEM] * 2)(vk, value_in[-1])
    own, share = call(
        value_prefix_kernel, [shape(*vk.shape)] * 2, [VMEM] * (rounds + 1)
    )(keep, near, *value_in)
    far = swap(share, "seq", size, 1)

    mat, ridges, norms, *state = call(
        functools.partial(cg_first_kernel, width, FIRST),
        [
            shape(heads, width, width),
            shape(heads, width, width, dtype=F32),
            shape(heads, toks, dtype=F32),
        ]
        + [shape(heads, width, toks, dtype=F32)] * 3,
        [VMEM] * 7,
        mib=4,
        flops=10 * work,
    )(keys, kt, qt, local, ridge_diag, key_own, key_far)
    x = call(
        functools.partial(cg_last_kernel, width, ITERS - 1 - FIRST),
        shape(toks, cols),
        [VMEM] * 8,
        [pltpu.VMEM((heads, width, toks), F32)] * 3,
        mib=8,
        flops=10 * work,
    )(keys, kt, mat, ridges, norms, *state)

    local = call(
        functools.partial(local_read_kernel, width),
        shape(toks, cols, dtype=F32),
        [VMEM] * 3,
        flops=work,
    )(x, keys, vals)
    pieces = call(
        functools.partial(read_kernel, width, spots),
        [shape(rows, cols)] * spots,
        [VMEM] * 4,
        [pltpu.VMEM((toks, cols), BF16)],
        flops=work,
    )(x, local, own, far)
    arrived = [pieces[0]] + [swap(pieces[k], "head", spots, k) for k in range(1, spots)]
    return call(
        functools.partial(norm_kernel, spots),
        shape(rows, spots * cols),
        [VMEM] * (spots + 1),
        flops=work,
    )(*arrived, gated)


def solution(mesh):
    return jax.shard_map(
        functools.partial(shards, mesh),
        mesh=mesh,
        in_specs=(
            P("seq", "head"),
            P("seq", "head"),
            P("seq", "head"),
            P("seq", "head"),
            P("head", None),
            P(),
            P(("seq", "head"), None),
        ),
        out_specs=P(("seq", "head"), None),
        check_vma=False,
    )
```

```python
import functools

import jax
import jax.numpy as jnp
from jax import lax
from jax.experimental import pallas as pl
from jax.experimental.pallas import tpu as pltpu
from jax.sharding import PartitionSpec as P


ITERS = 8
FIRST = 5
EPS = 1e-06

F32 = jnp.float32
BF16 = jnp.bfloat16
VMEM = pl.BlockSpec(memory_space=pltpu.VMEM)


def call(body, shapes, specs, scratch=(), mib=4, flops=0):
    single = not isinstance(shapes, list)
    return pl.pallas_call(
        body,
        out_shape=shapes,
        in_specs=specs,
        out_specs=VMEM if single else [VMEM] * len(shapes),
        scratch_shapes=list(scratch),
        compiler_params=pltpu.CompilerParams(vmem_limit_bytes=mib << 20),
        cost_estimate=pl.CostEstimate(flops=flops, bytes_accessed=1 << 20, transcendentals=0),
    )


def dot(a, b, dims=((1,), (0,))):
    return lax.dot_general(a, b, (dims, ((), ())), preferred_element_type=F32)


def square_sum(block, axis):
    return jnp.sum(block * block, axis=axis, keepdims=True)


def key_state_kernel(width, k_hbm, v_hbm, gate_hbm, keep_ref, give_ref, kt_ref, k_ref, v_ref, scale_ref, gate_ref, sems):
    heads = gate_ref.shape[0]
    half = width // 2
    loads = [pltpu.make_async_copy(gate_hbm, gate_ref, sems.at[0])]
    loads.append(pltpu.make_async_copy(k_hbm, k_ref, sems.at[1]))
    loads.append(pltpu.make_async_copy(v_hbm, v_ref, sems.at[2]))
    for load in loads:
        load.start()
    row = lax.broadcasted_iota(jnp.int32, (half, width), 0)
    col = lax.broadcasted_iota(jnp.int32, (half, width), 1)
    loads[0].wait()
    loads[1].wait()
    later = (lax.axis_index("seq") & 1) == 1
    count = heads // 2
    blocks, diags = [], []
    for h in range(heads):
        key = k_ref[:, h * width : (h + 1) * width]
        turned = key.T.astype(F32)
        total = square_sum(turned, 0) + EPS
        scale_ref[h : h + 1] = gate_ref[h : h + 1] * lax.rsqrt(total)
        wide = (turned * (gate_ref[h : h + 1] / total)).astype(BF16)
        kt_ref[h] = wide
        kk = dot(wide, key)
        diag = jnp.where(row == col, kk[:half], jnp.where(row + half == col, kk[half:], 0.0))
        diags.append(jnp.sum(diag, axis=0, keepdims=True))
        other = pltpu.roll(kk[half:], half, 1)
        packed = jnp.where(row > col, other, jnp.where(row == col, 0.0, kk[:half]))
        blocks.append(packed.astype(BF16))
    for h in range(count):
        rows = slice(h * half, (h + 1) * half)
        keep_ref[rows] = jnp.where(later, blocks[count + h], blocks[h])
        give_ref[rows] = jnp.where(later, blocks[h], blocks[count + h])
    low, high = jnp.concatenate(diags[:count], axis=0), jnp.concatenate(diags[count:], axis=0)
    store_diag(keep_ref, count * half, jnp.where(later, high, low))
    store_diag(give_ref, count * half, jnp.where(later, low, high))
    loads[2].wait()


def store_diag(ref, at, diag):
    heads = diag.shape[0]
    high = diag.astype(BF16)
    ref[at : at + 2 * heads] = jnp.concatenate(
        [high, (diag - high.astype(F32)).astype(BF16)], axis=0
    )


def load_diag(ref, at):
    both = ref[at:].astype(F32)
    heads = both.shape[0] // 2
    return both[:heads] + both[heads:]


def key_join_kernel(at, mine_ref, other_ref, total_ref):
    total_ref[:at] = (mine_ref[:at].astype(F32) + other_ref[:at].astype(F32)).astype(BF16)
    store_diag(total_ref, at, load_diag(mine_ref, at) + load_diag(other_ref, at))


def key_prefix_kernel(at, keep_ref, near_ref, *refs):
    later = (lax.axis_index("seq") & 1).astype(F32)
    for load, store in (
        (lambda ref: ref[:at].astype(F32), lambda ref, x: ref.__setitem__(slice(0, at), x.astype(BF16))),
        (lambda ref: load_diag(ref, at), lambda ref, x: store_diag(ref, at, x)),
    ):
        before = prefix(refs[:-2], load, 1)
        store(refs[-2], before + later * load(near_ref))
        store(refs[-1], before + (1.0 - later) * load(keep_ref))


def value_join_kernel(mine_ref, other_ref, total_ref):
    total_ref[...] = (mine_ref[...].astype(F32) + other_ref[...].astype(F32)).astype(BF16)


def value_prefix_kernel(keep_ref, near_ref, *refs):
    later = (lax.axis_index("seq") & 1).astype(F32)
    before = prefix(refs[:-2], lambda ref: ref[...].astype(F32), 1)
    refs[-2][...] = (before + later * near_ref[...].astype(F32)).astype(BF16)
    refs[-1][...] = (before + (1.0 - later) * keep_ref[...].astype(F32)).astype(BF16)


def value_state_kernel(width, k_ref, v_ref, scale_ref, val_ref, keep_ref, give_ref):
    scales = scale_ref[...].T
    later = (lax.axis_index("seq") & 1) == 1
    count = keep_ref.shape[0]
    for h in range(count):
        pair = []
        for head in (h, count + h):
            cols = slice(head * width, (head + 1) * width)
            val = (v_ref[:, cols].astype(F32) * scales[:, head : head + 1]).astype(BF16)
            val_ref[:, cols] = val
            pair.append(dot(val, k_ref[:, cols], ((0,), (0,))))
        keep_ref[h] = jnp.where(later, pair[1], pair[0]).astype(BF16)
        give_ref[h] = jnp.where(later, pair[0], pair[1]).astype(BF16)


def causal(k_ref, low, h):
    width, toks = low.shape
    half = toks // 2
    score = dot(k_ref[:, h * width : (h + 1) * width], low).astype(BF16)
    keep = lax.broadcasted_iota(jnp.int32, (half, half), 0) <= lax.broadcasted_iota(
        jnp.int32, (half, half), 1
    )
    none = jnp.zeros((half, half), BF16)
    upper = jnp.concatenate([jnp.where(keep, score[:half, :half], none), score[:half, half:]], axis=1)
    lower = jnp.concatenate([none, jnp.where(keep, score[half:, half:], none)], axis=1)
    return [upper, lower]


def prepare_kernel(width, q_ref, k_ref, kt_ref, qt_ref, local_ref):
    for h in range(qt_ref.shape[0]):
        query = q_ref[:, h * width : (h + 1) * width].T.astype(F32)
        query = query * lax.rsqrt(square_sum(query, 0) + EPS)
        qt_ref[h] = query
        scores = jnp.concatenate(causal(k_ref, query.astype(BF16), h), axis=0)
        local_ref[h] = dot(kt_ref[h], scores)


def gate_kernel(gain_ref, logit_ref, out_ref):
    out_ref[...] = gain_ref[...] * jax.nn.sigmoid(logit_ref[...].astype(F32))


def prefix(refs, load, first=0):
    place = lax.axis_index("seq")
    total = 0.0
    for k, ref in enumerate(refs):
        total = total + load(ref) * ((place >> (first + k)) & 1).astype(F32)
    return total


def operator(k_ref, kt_ref, mat_ref, directions, h):
    low = directions[h].astype(BF16)
    both = jnp.concatenate([mat_ref[h], kt_ref[h]], axis=1)
    return dot(both, jnp.concatenate([low] + causal(k_ref, low, h), axis=0))


def sweep(k_ref, kt_ref, mat_ref, ridges, old, new, norms, local=None):
    after = []
    width, toks = old[0].shape[1:]
    for h in range(mat_ref.shape[0]):
        if local is None:
            image = operator(k_ref, kt_ref, mat_ref, old[1], h)
        else:
            image = local[h] + dot(mat_ref[h], old[1][h].astype(BF16))
        parts = []
        for c in range(0, toks, width):
            at = slice(c, c + width)
            direction = old[1][h, :, at]
            applied = image[:, at] + ridges[h] * direction
            norm = norms[h][:, at]
            alpha = norm / jnp.sum(direction * applied, axis=0, keepdims=True)
            residual = old[0][h, :, at] - alpha * applied
            new[0][h, :, at] = residual
            following = square_sum(residual, 0)
            step = alpha * direction
            new[2][h, :, at] = step if old[2] is None else old[2][h, :, at] + step
            new[1][h, :, at] = residual + (following / norm) * direction
            parts.append(following)
        after.append(jnp.concatenate(parts, axis=1))
    return tuple(after)


def cg_first_kernel(width, sweeps, k_ref, kt_ref, qt_ref, local_ref, ridge_ref, own_ref, far_ref, *refs):
    mat_ref, ridges, norm_ref, *state = refs
    heads, _, _ = qt_ref.shape
    part = width // 2
    inner = lax.broadcasted_iota(jnp.int32, (part, part), 0) < lax.broadcasted_iota(
        jnp.int32, (part, part), 1
    )
    count = heads // 2
    own_diag, far_diag = load_diag(own_ref, count * part), load_diag(far_ref, count * part)
    later = (lax.axis_index("seq") & 1) == 1
    low = jnp.where(later, far_diag, own_diag)
    high = jnp.where(later, own_diag, far_diag)
    ridge_t = (ridge_ref[...] + jnp.concatenate([low, high], axis=0)).T
    norms = []
    for h in range(heads):
        rows = slice(h % count * part, (h % count + 1) * part)
        first, second = (own_ref, far_ref) if h < count else (far_ref, own_ref)
        upper = jnp.where(later, second[rows], first[rows]).astype(F32)
        turned = upper.T
        tri = upper[:, :part]
        tri_t = turned[:part]
        mat_ref[h, :part] = jnp.concatenate(
            [jnp.where(inner, tri, tri_t), upper[:, part:]], axis=1
        ).astype(BF16)
        mat_ref[h, part:] = jnp.concatenate(
            [turned[part:], jnp.where(inner, tri_t, tri)], axis=1
        ).astype(BF16)
        ridges[h] = jnp.broadcast_to(ridge_t[:, h : h + 1], (width, width))
        norms.append(square_sum(qt_ref[h], 0))
    fixed = (k_ref, kt_ref, mat_ref, ridges)
    norms = sweep(*fixed, (qt_ref, qt_ref, None), state, norms, local_ref)
    norms = lax.fori_loop(1, sweeps, lambda _, now: sweep(*fixed, state, state, now), norms, unroll=True)
    norm_ref[...] = jnp.concatenate(norms, axis=0)


def cg_last_kernel(width, sweeps, k_ref, kt_ref, mat_ref, ridges, norm_ref, *refs):
    given, x_ref, state = refs[:3], refs[3], refs[4:]
    heads = mat_ref.shape[0]
    fixed = (k_ref, kt_ref, mat_ref, ridges)
    norms = tuple(norm_ref[h : h + 1] for h in range(heads))
    norms = sweep(*fixed, given, state, norms)
    norms = lax.fori_loop(1, sweeps, lambda _, now: sweep(*fixed, state, state, now), norms, unroll=True)
    for h in range(heads):
        direction = state[1][h]
        ridge = jnp.concatenate([ridges[h]] * (direction.shape[1] // width), axis=1)
        image = operator(k_ref, kt_ref, mat_ref, state[1], h) + ridge * direction
        alpha = norms[h] / jnp.sum(direction * image, axis=0, keepdims=True)
        x = state[2][h] + alpha * direction
        x_ref[:, h * width : (h + 1) * width] = x.astype(BF16).T


def local_read_kernel(width, x_ref, k_ref, val_ref, local_ref):
    toks = k_ref.shape[0]
    keep = lax.broadcasted_iota(jnp.int32, (toks, toks), 0) >= lax.broadcasted_iota(
        jnp.int32, (toks, toks), 1
    )
    for h in range(k_ref.shape[1] // width):
        cols = slice(h * width, (h + 1) * width)
        score = jnp.where(keep, dot(x_ref[:, cols], k_ref[:, cols], ((1,), (1,))), 0.0)
        local_ref[:, cols] = dot(score.astype(BF16), val_ref[:, cols])


def read_kernel(width, spots, x_ref, local_ref, own_ref, far_ref, *refs):
    outs, tmp = refs[:spots], refs[spots]
    count = own_ref.shape[0]
    later = lax.axis_index("seq") & 1
    rows = x_ref.shape[0] // spots
    me = lax.axis_index("head")
    for h in range(x_ref.shape[1] // width):
        cols = slice(h * width, (h + 1) * width)
        state = jnp.where(later == h // count, own_ref[h % count], far_ref[h % count])
        out = dot(x_ref[:, cols], state, ((1,), (1,))) + local_ref[:, cols]
        tmp[:, cols] = out.astype(BF16)
    for k in range(spots):
        outs[k][...] = tmp[pl.ds(pl.multiple_of((me ^ k) * rows, rows), rows), :]


def norm_kernel(spots, *refs):
    pieces, gate_ref, out_ref = refs[:spots], refs[spots], refs[spots + 1]
    me = lax.axis_index("head")
    wide = pieces[0].shape[1]
    total = 0.0
    for k in range(spots):
        total = total + square_sum(pieces[k][...].astype(F32), 1)
    factor = lax.rsqrt(total / (wide * spots) + EPS)
    for k in range(spots):
        cols = pl.ds(pl.multiple_of((me ^ k) * wide, wide), wide)
        out_ref[:, cols] = (pieces[k][...].astype(F32) * factor * gate_ref[:, cols]).astype(BF16)


def swap(x, axis, size, step):
    return lax.ppermute(x, axis, [(i, i ^ step) for i in range(size)])


def route(k):
    return [1 << b for b in reversed(range(k.bit_length())) if k >> b & 1]


def shape(*dims, dtype=BF16):
    return jax.ShapeDtypeStruct(dims, dtype)


def shards(mesh, queries, key_rows, values, write_gate, ridge_diag, norm_gain, gate_logits):
    toks, cols = queries.shape
    heads = write_gate.shape[1]
    width = cols // heads
    spots = mesh.shape["head"]
    size = mesh.shape["seq"]
    rounds = size.bit_length() - 1
    rows = toks // spots
    gates = write_gate.T
    tall = heads // 2 * width // 2
    packed = tall + heads
    work = 2 * toks * width * width * heads

    keep, give, kt, keys, vals, scales = call(
        functools.partial(key_state_kernel, width),
        [
            shape(packed, width),
            shape(packed, width),
            shape(heads, width, toks),
            shape(toks, cols),
            shape(toks, cols),
            shape(heads, toks, dtype=F32),
        ],
        [pl.BlockSpec(memory_space=pltpu.MemorySpace.HBM)] * 3,
        [pltpu.VMEM((heads, toks), F32), pltpu.SemaphoreType.DMA((3,))],
        flops=work,
    )(
        *(
            pltpu.with_memory_space_constraint(x, pltpu.MemorySpace.HBM)
            for x in (key_rows, values, gates)
        )
    )
    vals, value_keep, value_give = call(
        functools.partial(value_state_kernel, width),
        [shape(toks, cols)] + [shape(heads // 2, width, width)] * 2,
        [VMEM] * 3,
        flops=work,
    )(keys, vals, scales)
    qt, local = call(
        functools.partial(prepare_kernel, width),
        [shape(heads, width, toks, dtype=F32)] * 2,
        [VMEM] * 3,
        mib=4,
        flops=work,
    )(queries, keys, kt)
    gated = call(gate_kernel, shape(*gate_logits.shape, dtype=F32), [VMEM] * 2, flops=work)(
        norm_gain[None, :], gate_logits
    )

    key_in, value_in = [], []
    near = swap(give, "seq", size, 1)
    kk = keep
    for k in range(1, rounds):
        kk = call(
            functools.partial(key_join_kernel, tall), shape(packed, width), [VMEM] * 2
        )(kk, key_in[-1] if key_in else near)
        key_in.append(swap(kk, "seq", size, 1 << k))
    key_own, share = call(
        functools.partial(key_prefix_kernel, tall),
        [shape(packed, width)] * 2,
        [VMEM] * (rounds + 1),
    )(keep, near, *key_in)
    key_far = swap(share, "seq", size, 1)

    keep = value_keep
    near = swap(value_give, "seq", size, 1)
    vk = call(value_join_kernel, shape(*keep.shape), [VMEM] * 2)(keep, near)
    for k in range(1, rounds):
        value_in.append(swap(vk, "seq", size, 1 << k))
        if k + 1 < rounds:
            vk = call(value_join_kernel, shape(*vk.shape), [VMEM] * 2)(vk, value_in[-1])
    own, share = call(
        value_prefix_kernel, [shape(*vk.shape)] * 2, [VMEM] * (rounds + 1)
    )(keep, near, *value_in)
    far = swap(share, "seq", size, 1)

    mat, ridges, norms, *state = call(
        functools.partial(cg_first_kernel, width, FIRST),
        [
            shape(heads, width, width),
            shape(heads, width, width, dtype=F32),
            shape(heads, toks, dtype=F32),
        ]
        + [shape(heads, width, toks, dtype=F32)] * 3,
        [VMEM] * 7,
        mib=4,
        flops=10 * work,
    )(keys, kt, qt, local, ridge_diag, key_own, key_far)
    x = call(
        functools.partial(cg_last_kernel, width, ITERS - 1 - FIRST),
        shape(toks, cols),
        [VMEM] * 8,
        [pltpu.VMEM((heads, width, toks), F32)] * 3,
        mib=8,
        flops=10 * work,
    )(keys, kt, mat, ridges, norms, *state)

    local = call(
        functools.partial(local_read_kernel, width),
        shape(toks, cols, dtype=F32),
        [VMEM] * 3,
        flops=work,
    )(x, keys, vals)
    pieces = call(
        functools.partial(read_kernel, width, spots),
        [shape(rows, cols)] * spots,
        [VMEM] * 4,
        [pltpu.VMEM((toks, cols), BF16)],
        flops=work,
    )(x, local, own, far)
    arrived = [pieces[0]]
    for k in range(1, spots):
        piece = pieces[k]
        for hop in route(k):
            piece = swap(piece, "head", spots, hop)
        arrived.append(piece)
    return call(
        functools.partial(norm_kernel, spots),
        shape(rows, spots * cols),
        [VMEM] * (spots + 1),
        flops=work,
    )(*arrived, gated)


def solution(mesh):
    return jax.shard_map(
        functools.partial(shards, mesh),
        mesh=mesh,
        in_specs=(
            P("seq", "head"),
            P("seq", "head"),
            P("seq", "head"),
            P("seq", "head"),
            P("head", None),
            P(),
            P(("seq", "head"), None),
        ),
        out_specs=P(("seq", "head"), None),
        check_vma=False,
    )
```

```python
import functools

import jax
import jax.numpy as jnp
from jax import lax
from jax.experimental import pallas as pl
from jax.experimental.pallas import tpu as pltpu
from jax.sharding import PartitionSpec as P


ITERS = 8
FIRST = 5
EPS = 1e-06

F32 = jnp.float32
BF16 = jnp.bfloat16
VMEM = pl.BlockSpec(memory_space=pltpu.VMEM)


def call(body, shapes, specs, scratch=(), mib=4, flops=0):
    single = not isinstance(shapes, list)
    return pl.pallas_call(
        body,
        out_shape=shapes,
        in_specs=specs,
        out_specs=VMEM if single else [VMEM] * len(shapes),
        scratch_shapes=list(scratch),
        compiler_params=pltpu.CompilerParams(vmem_limit_bytes=mib << 20),
        cost_estimate=pl.CostEstimate(flops=flops, bytes_accessed=1 << 20, transcendentals=0),
    )


def dot(a, b, dims=((1,), (0,))):
    return lax.dot_general(a, b, (dims, ((), ())), preferred_element_type=F32)


def square_sum(block, axis):
    return jnp.sum(block * block, axis=axis, keepdims=True)


def key_state_kernel(width, k_hbm, v_hbm, gate_hbm, keep_ref, give_ref, kt_ref, k_ref, v_ref, scale_ref, gate_ref, sems):
    heads = gate_ref.shape[0]
    half = width // 2
    loads = [pltpu.make_async_copy(gate_hbm, gate_ref, sems.at[0])]
    loads.append(pltpu.make_async_copy(k_hbm, k_ref, sems.at[1]))
    loads.append(pltpu.make_async_copy(v_hbm, v_ref, sems.at[2]))
    for load in loads:
        load.start()
    row = lax.broadcasted_iota(jnp.int32, (half, width), 0)
    col = lax.broadcasted_iota(jnp.int32, (half, width), 1)
    loads[0].wait()
    loads[1].wait()
    later = (lax.axis_index("seq") & 1) == 1
    count = heads // 2
    blocks, diags = [], []
    for h in range(heads):
        key = k_ref[:, h * width : (h + 1) * width]
        turned = key.T.astype(F32)
        total = square_sum(turned, 0) + EPS
        scale_ref[h : h + 1] = gate_ref[h : h + 1] * lax.rsqrt(total)
        wide = (turned * (gate_ref[h : h + 1] / total)).astype(BF16)
        kt_ref[h] = wide
        kk = dot(wide, key)
        diag = jnp.where(row == col, kk[:half], jnp.where(row + half == col, kk[half:], 0.0))
        diags.append(jnp.sum(diag, axis=0, keepdims=True))
        other = pltpu.roll(kk[half:], half, 1)
        packed = jnp.where(row > col, other, jnp.where(row == col, 0.0, kk[:half]))
        blocks.append(packed.astype(BF16))
    for h in range(count):
        rows = slice(h * half, (h + 1) * half)
        keep_ref[rows] = jnp.where(later, blocks[count + h], blocks[h])
        give_ref[rows] = jnp.where(later, blocks[h], blocks[count + h])
    low, high = jnp.concatenate(diags[:count], axis=0), jnp.concatenate(diags[count:], axis=0)
    store_diag(keep_ref, count * half, jnp.where(later, high, low))
    store_diag(give_ref, count * half, jnp.where(later, low, high))
    loads[2].wait()


def store_diag(ref, at, diag):
    heads = diag.shape[0]
    high = diag.astype(BF16)
    ref[at : at + 2 * heads] = jnp.concatenate(
        [high, (diag - high.astype(F32)).astype(BF16)], axis=0
    )


def load_diag(ref, at):
    both = ref[at:].astype(F32)
    heads = both.shape[0] // 2
    return both[:heads] + both[heads:]


def key_join_kernel(at, mine_ref, other_ref, total_ref):
    total_ref[:at] = (mine_ref[:at].astype(F32) + other_ref[:at].astype(F32)).astype(BF16)
    store_diag(total_ref, at, load_diag(mine_ref, at) + load_diag(other_ref, at))


def key_prefix_kernel(at, keep_ref, near_ref, *refs):
    later = (lax.axis_index("seq") & 1).astype(F32)
    for load, store in (
        (lambda ref: ref[:at].astype(F32), lambda ref, x: ref.__setitem__(slice(0, at), x.astype(BF16))),
        (lambda ref: load_diag(ref, at), lambda ref, x: store_diag(ref, at, x)),
    ):
        before = prefix(refs[:-2], load, 1)
        store(refs[-2], before + later * load(near_ref))
        store(refs[-1], before + (1.0 - later) * load(keep_ref))


def value_join_kernel(mine_ref, other_ref, total_ref):
    total_ref[...] = (mine_ref[...].astype(F32) + other_ref[...].astype(F32)).astype(BF16)


def value_prefix_kernel(keep_ref, near_ref, *refs):
    later = (lax.axis_index("seq") & 1).astype(F32)
    before = prefix(refs[:-2], lambda ref: ref[...].astype(F32), 1)
    refs[-2][...] = (before + later * near_ref[...].astype(F32)).astype(BF16)
    refs[-1][...] = (before + (1.0 - later) * keep_ref[...].astype(F32)).astype(BF16)


def value_state_kernel(width, k_ref, v_ref, scale_ref, val_ref, keep_ref, give_ref):
    scales = scale_ref[...].T
    later = (lax.axis_index("seq") & 1) == 1
    count = keep_ref.shape[0]
    for h in range(count):
        pair = []
        for head in (h, count + h):
            cols = slice(head * width, (head + 1) * width)
            val = (v_ref[:, cols].astype(F32) * scales[:, head : head + 1]).astype(BF16)
            val_ref[:, cols] = val
            pair.append(dot(val, k_ref[:, cols], ((0,), (0,))))
        keep_ref[h] = jnp.where(later, pair[1], pair[0]).astype(BF16)
        give_ref[h] = jnp.where(later, pair[0], pair[1]).astype(BF16)


def causal(k_ref, low, h):
    width, toks = low.shape
    half = toks // 2
    score = dot(k_ref[:, h * width : (h + 1) * width], low).astype(BF16)
    keep = lax.broadcasted_iota(jnp.int32, (half, half), 0) <= lax.broadcasted_iota(
        jnp.int32, (half, half), 1
    )
    none = jnp.zeros((half, half), BF16)
    upper = jnp.concatenate([jnp.where(keep, score[:half, :half], none), score[:half, half:]], axis=1)
    lower = jnp.concatenate([none, jnp.where(keep, score[half:, half:], none)], axis=1)
    return [upper, lower]


def prepare_kernel(width, q_ref, k_ref, kt_ref, qt_ref, local_ref):
    for h in range(qt_ref.shape[0]):
        query = q_ref[:, h * width : (h + 1) * width].T.astype(F32)
        query = query * lax.rsqrt(square_sum(query, 0) + EPS)
        qt_ref[h] = query
        scores = jnp.concatenate(causal(k_ref, query.astype(BF16), h), axis=0)
        local_ref[h] = dot(kt_ref[h], scores)


def gate_kernel(gain_ref, logit_ref, out_ref):
    out_ref[...] = gain_ref[...] * jax.nn.sigmoid(logit_ref[...].astype(F32))


def prefix(refs, load, first=0):
    place = lax.axis_index("seq")
    total = 0.0
    for k, ref in enumerate(refs):
        total = total + load(ref) * ((place >> (first + k)) & 1).astype(F32)
    return total


def operator(k_ref, kt_ref, mat_ref, directions, h):
    low = directions[h].astype(BF16)
    both = jnp.concatenate([mat_ref[h], kt_ref[h]], axis=1)
    return dot(both, jnp.concatenate([low] + causal(k_ref, low, h), axis=0))


def sweep(k_ref, kt_ref, mat_ref, ridges, old, new, norms, local=None, final=False):
    after = []
    width, toks = old[0].shape[1:]
    for h in range(mat_ref.shape[0]):
        if local is None:
            image = operator(k_ref, kt_ref, mat_ref, old[1], h)
        else:
            image = local[h] + dot(mat_ref[h], old[1][h].astype(BF16))
        parts = []
        for c in range(0, toks, width):
            at = slice(c, c + width)
            direction = old[1][h, :, at]
            applied = image[:, at] + ridges[h] * direction
            norm = norms[h][:, at]
            alpha = norm / jnp.sum(direction * applied, axis=0, keepdims=True)
            residual = old[0][h, :, at] - alpha * applied
            if not final:
                new[0][h, :, at] = residual
            following = square_sum(residual, 0)
            step = alpha * direction
            new[2][h, :, at] = step if old[2] is None else old[2][h, :, at] + step
            new[1][h, :, at] = residual + (following / norm) * direction
            parts.append(following)
        after.append(jnp.concatenate(parts, axis=1))
    return tuple(after)


def cg_first_kernel(width, sweeps, k_ref, kt_ref, qt_ref, local_ref, ridge_ref, own_ref, far_ref, *refs):
    mat_ref, ridges, norm_ref, *state = refs
    heads, _, _ = qt_ref.shape
    part = width // 2
    inner = lax.broadcasted_iota(jnp.int32, (part, part), 0) < lax.broadcasted_iota(
        jnp.int32, (part, part), 1
    )
    count = heads // 2
    own_diag, far_diag = load_diag(own_ref, count * part), load_diag(far_ref, count * part)
    later = (lax.axis_index("seq") & 1) == 1
    low = jnp.where(later, far_diag, own_diag)
    high = jnp.where(later, own_diag, far_diag)
    ridge_t = (ridge_ref[...] + jnp.concatenate([low, high], axis=0)).T
    norms = []
    for h in range(heads):
        rows = slice(h % count * part, (h % count + 1) * part)
        first, second = (own_ref, far_ref) if h < count else (far_ref, own_ref)
        upper = jnp.where(later, second[rows], first[rows]).astype(F32)
        turned = upper.T
        tri = upper[:, :part]
        tri_t = turned[:part]
        mat_ref[h, :part] = jnp.concatenate(
            [jnp.where(inner, tri, tri_t), upper[:, part:]], axis=1
        ).astype(BF16)
        mat_ref[h, part:] = jnp.concatenate(
            [turned[part:], jnp.where(inner, tri_t, tri)], axis=1
        ).astype(BF16)
        ridges[h] = jnp.broadcast_to(ridge_t[:, h : h + 1], (width, width))
        norms.append(square_sum(qt_ref[h], 0))
    fixed = (k_ref, kt_ref, mat_ref, ridges)
    norms = sweep(*fixed, (qt_ref, qt_ref, None), state, norms, local_ref)
    norms = lax.fori_loop(1, sweeps, lambda _, now: sweep(*fixed, state, state, now), norms, unroll=True)
    norm_ref[...] = jnp.concatenate(norms, axis=0)


def cg_last_kernel(width, sweeps, k_ref, kt_ref, mat_ref, ridges, norm_ref, *refs):
    given, x_ref, state = refs[:3], refs[3], refs[4:]
    heads = mat_ref.shape[0]
    fixed = (k_ref, kt_ref, mat_ref, ridges)
    norms = tuple(norm_ref[h : h + 1] for h in range(heads))
    for turn in range(sweeps):
        norms = sweep(*fixed, state if turn else given, state, norms, final=turn + 1 == sweeps)
    for h in range(heads):
        direction = state[1][h]
        ridge = jnp.concatenate([ridges[h]] * (direction.shape[1] // width), axis=1)
        image = operator(k_ref, kt_ref, mat_ref, state[1], h) + ridge * direction
        alpha = norms[h] / jnp.sum(direction * image, axis=0, keepdims=True)
        x = state[2][h] + alpha * direction
        x_ref[:, h * width : (h + 1) * width] = x.astype(BF16).T


def local_read_kernel(width, x_ref, k_ref, val_ref, local_ref):
    toks = k_ref.shape[0]
    keep = lax.broadcasted_iota(jnp.int32, (toks, toks), 0) >= lax.broadcasted_iota(
        jnp.int32, (toks, toks), 1
    )
    for h in range(k_ref.shape[1] // width):
        cols = slice(h * width, (h + 1) * width)
        score = jnp.where(keep, dot(x_ref[:, cols], k_ref[:, cols], ((1,), (1,))), 0.0)
        local_ref[:, cols] = dot(score.astype(BF16), val_ref[:, cols])


def read_kernel(width, spots, x_ref, local_ref, own_ref, far_ref, *refs):
    outs, tmp = refs[:spots], refs[spots]
    count = own_ref.shape[0]
    later = lax.axis_index("seq") & 1
    rows = x_ref.shape[0] // spots
    me = lax.axis_index("head")
    for h in range(x_ref.shape[1] // width):
        cols = slice(h * width, (h + 1) * width)
        state = jnp.where(later == h // count, own_ref[h % count], far_ref[h % count])
        out = dot(x_ref[:, cols], state, ((1,), (1,))) + local_ref[:, cols]
        tmp[:, cols] = out.astype(BF16)
    for k in range(spots):
        outs[k][...] = tmp[pl.ds(pl.multiple_of((me ^ k) * rows, rows), rows), :]


def norm_kernel(spots, *refs):
    pieces, gate_ref, out_ref = refs[:spots], refs[spots], refs[spots + 1]
    me = lax.axis_index("head")
    wide = pieces[0].shape[1]
    total = 0.0
    for k in range(spots):
        total = total + square_sum(pieces[k][...].astype(F32), 1)
    factor = lax.rsqrt(total / (wide * spots) + EPS)
    for k in range(spots):
        cols = pl.ds(pl.multiple_of((me ^ k) * wide, wide), wide)
        out_ref[:, cols] = (pieces[k][...].astype(F32) * factor * gate_ref[:, cols]).astype(BF16)


def swap(x, axis, size, step):
    return lax.ppermute(x, axis, [(i, i ^ step) for i in range(size)])


def route(k):
    return [1 << b for b in reversed(range(k.bit_length())) if k >> b & 1]


def shape(*dims, dtype=BF16):
    return jax.ShapeDtypeStruct(dims, dtype)


def shards(mesh, queries, key_rows, values, write_gate, ridge_diag, norm_gain, gate_logits):
    toks, cols = queries.shape
    heads = write_gate.shape[1]
    width = cols // heads
    spots = mesh.shape["head"]
    size = mesh.shape["seq"]
    rounds = size.bit_length() - 1
    rows = toks // spots
    gates = write_gate.T
    tall = heads // 2 * width // 2
    packed = tall + heads
    work = 2 * toks * width * width * heads

    keep, give, kt, keys, vals, scales = call(
        functools.partial(key_state_kernel, width),
        [
            shape(packed, width),
            shape(packed, width),
            shape(heads, width, toks),
            shape(toks, cols),
            shape(toks, cols),
            shape(heads, toks, dtype=F32),
        ],
        [pl.BlockSpec(memory_space=pltpu.MemorySpace.HBM)] * 3,
        [pltpu.VMEM((heads, toks), F32), pltpu.SemaphoreType.DMA((3,))],
        flops=work,
    )(
        *(
            pltpu.with_memory_space_constraint(x, pltpu.MemorySpace.HBM)
            for x in (key_rows, values, gates)
        )
    )
    vals, value_keep, value_give = call(
        functools.partial(value_state_kernel, width),
        [shape(toks, cols)] + [shape(heads // 2, width, width)] * 2,
        [VMEM] * 3,
        flops=work,
    )(keys, vals, scales)
    qt, local = call(
        functools.partial(prepare_kernel, width),
        [shape(heads, width, toks, dtype=F32)] * 2,
        [VMEM] * 3,
        mib=4,
        flops=work,
    )(queries, keys, kt)
    gated = call(gate_kernel, shape(*gate_logits.shape, dtype=F32), [VMEM] * 2, flops=work)(
        norm_gain[None, :], gate_logits
    )

    key_in, value_in = [], []
    near = swap(give, "seq", size, 1)
    kk = keep
    for k in range(1, rounds):
        kk = call(
            functools.partial(key_join_kernel, tall), shape(packed, width), [VMEM] * 2
        )(kk, key_in[-1] if key_in else near)
        key_in.append(swap(kk, "seq", size, 1 << k))
    key_own, share = call(
        functools.partial(key_prefix_kernel, tall),
        [shape(packed, width)] * 2,
        [VMEM] * (rounds + 1),
    )(keep, near, *key_in)
    key_far = swap(share, "seq", size, 1)

    keep = value_keep
    near = swap(value_give, "seq", size, 1)
    vk = call(value_join_kernel, shape(*keep.shape), [VMEM] * 2)(keep, near)
    for k in range(1, rounds):
        value_in.append(swap(vk, "seq", size, 1 << k))
        if k + 1 < rounds:
            vk = call(value_join_kernel, shape(*vk.shape), [VMEM] * 2)(vk, value_in[-1])
    own, share = call(
        value_prefix_kernel, [shape(*vk.shape)] * 2, [VMEM] * (rounds + 1)
    )(keep, near, *value_in)
    far = swap(share, "seq", size, 1)

    mat, ridges, norms, *state = call(
        functools.partial(cg_first_kernel, width, FIRST),
        [
            shape(heads, width, width),
            shape(heads, width, width, dtype=F32),
            shape(heads, toks, dtype=F32),
        ]
        + [shape(heads, width, toks, dtype=F32)] * 3,
        [VMEM] * 7,
        mib=4,
        flops=10 * work,
    )(keys, kt, qt, local, ridge_diag, key_own, key_far)
    x = call(
        functools.partial(cg_last_kernel, width, ITERS - 1 - FIRST),
        shape(toks, cols),
        [VMEM] * 8,
        [pltpu.VMEM((heads, width, toks), F32)] * 3,
        mib=8,
        flops=10 * work,
    )(keys, kt, mat, ridges, norms, *state)

    local = call(
        functools.partial(local_read_kernel, width),
        shape(toks, cols, dtype=F32),
        [VMEM] * 3,
        flops=work,
    )(x, keys, vals)
    pieces = call(
        functools.partial(read_kernel, width, spots),
        [shape(rows, cols)] * spots,
        [VMEM] * 4,
        [pltpu.VMEM((toks, cols), BF16)],
        flops=work,
    )(x, local, own, far)
    arrived = [pieces[0]]
    for k in range(1, spots):
        piece = pieces[k]
        for hop in route(k):
            piece = swap(piece, "head", spots, hop)
        arrived.append(piece)
    return call(
        functools.partial(norm_kernel, spots),
        shape(rows, spots * cols),
        [VMEM] * (spots + 1),
        flops=work,
    )(*arrived, gated)


def solution(mesh):
    return jax.shard_map(
        functools.partial(shards, mesh),
        mesh=mesh,
        in_specs=(
            P("seq", "head"),
            P("seq", "head"),
            P("seq", "head"),
            P("seq", "head"),
            P("head", None),
            P(),
            P(("seq", "head"), None),
        ),
        out_specs=P(("seq", "head"), None),
        check_vma=False,
    )
```
